32 devices in a mesh: dp: 4 (over z), latent: 8 (over y, x, core).
Axes of the slice: x: 2, y: 2, z: 4, core: 2. Of those that a mesh axis runs over, the one named last changes fastest.
Arguments:
- inputs: bfloat16 [64, 2048], P(('dp', 'latent')), may hold values from -6 to 6
- blocks: int32 [64, 4], P(('dp', 'latent')), may hold values from 0 to 127, all different within a row; in each aligned block of 16 rows (0 to 15, 16 to 31, ...) at most 2 rows name the same one
- weights: bfloat16 [8192, 2048], P('latent'), as said below
- enc_bias: float32 [8192], P('latent'), may hold values from -3 to 3
- dec_bias: float32 [2048], replicated, may hold values from -3 to 3
Outputs:
- recon: bfloat16 [64, 2048], P(('dp', 'latent'))
- grad_weights: float32 [8192, 2048], P('latent', 'dp')
- block_scores: float32 [128, 64], P('latent', 'dp')
The draws below stay inside these ranges and needn't reach their ends.
Inputs may be any that keep to these rules, and one draw needn't show every extreme that they name: Each row names 4 different blocks. Within the rows of one data group (aligned runs of 16 rows) no block is named by more than 2 rows, and some block is named by exactly 2 rows. `weights`: rows have different lengths.
All inputs are finite; a program needn't handle non-finite values.
Results may differ from the reference program's by a relative error of at most 0.0068.
Values may be sent and summed in bfloat16 or wider, within the bound.
No kernel may reach another device: no remote copies, remote signals or barrier semaphores. Data moves between devices by JAX's collectives and lax.ppermute only.
A program may use at most 64 MiB of HBM per device.

```python
import math
import jax
import jax.numpy as jnp
import numpy as np
from jax import lax

D = 2048
LAT_DEV = 1024
BLK = 64
K = 4
ROW_DEV = 2
CAP = 2
NB = 128
LATENTS = 8192
ROWS_G = 16
TOTAL = 64
N_DP = 4
N_LATENT = 8


def draw_weights(key, part):
    key_scale, key_base = jax.random.split(key)
    row_scale = jnp.exp(jax.random.uniform(key_scale, (LATENTS, 1), jnp.float32, math.log(0.5), math.log(5.0)))
    base = jax.random.normal(key_base, (LATENTS, D), jnp.float32)
    return (base * row_scale / math.sqrt(D)).astype(jnp.bfloat16)


def block_levels(rng, extent, cuts, low, largest):
    level = 1.0
    for axis_at, blocks in cuts:
        draws = jax.random.uniform(jax.random.fold_in(jax.random.fold_in(rng, 6), axis_at), (blocks,), jnp.float32, low / len(cuts), largest / len(cuts))
        level = level * jnp.repeat(jnp.exp(draws), extent[axis_at] // blocks).reshape((-1,) + (1,) * (len(extent) - 1 - axis_at))
    return level


def assign_block(own_key, own, number, rows, number_of, top, reach, skew):
    sequence = jax.random.permutation(own_key, number_of)
    heavy_load, common = portions_of(number_of, rows * top, reach, skew, True), portions_of(number_of, rows * top, reach, skew, False)
    places = jnp.arange(number_of)

    def named(sizes, offset_by):
        used = int((sizes > 0).sum())
        fixed = max(1, used // 4)
        shifted = fixed + (places - fixed + offset_by * (used - fixed)) % max(1, number_of - fixed)
        return jnp.zeros((number_of,), jnp.int32).at[sequence[jnp.where(places < fixed, places, shifted)]].set(jnp.asarray(sizes, jnp.int32))

    sizes = jnp.where(number % 4 == 0, named(heavy_load, number // 4), named(common, number - number // 4 - 1))
    mixed = jax.random.permutation(jax.random.fold_in(own, 3), number_of)
    source_of, receiver = mixed[0:number_of // 2 * 2:2], mixed[1:number_of // 2 * 2:2]
    margin = jnp.minimum(sizes[source_of] - 1, reach - sizes[receiver]) // 2
    margin = jnp.where((source_of == sequence[0]) | (receiver == sequence[0]) | (sizes[receiver] == 0), 0, jnp.maximum(margin, 0))
    shifted = jax.random.randint(jax.random.fold_in(own, 4), (number_of // 2,), 0, 1 << 20) % (margin + 1)
    sizes = sizes.at[source_of].add(-shifted).at[receiver].add(shifted)
    items = jnp.searchsorted(jnp.cumsum(sizes), jnp.arange(rows * top), side="right").astype(jnp.int32)
    listing = items.reshape(top, rows).T
    listing = listing[jax.random.permutation(jax.random.fold_in(own, 1), rows)]
    offset_by = jax.random.randint(jax.random.fold_in(own, 2), (rows, 1), 0, top)
    return jnp.take_along_axis(listing, (jnp.arange(top)[None, :] + offset_by) % top, axis=1)


def portions_of(count, total, bound, skew, full):
    portions = [(1 << 20) // math.isqrt(standing ** skew) + 1 for standing in range(1, count + 1)]
    largest = bound if full else min(bound, max(-(-total // count), total * portions[0] // sum(portions)))
    least = 1 if total - largest >= count - 1 else 0
    given, surplus = [largest] + [least] * (count - 1), total - largest - least * (count - 1)
    while surplus > 0:
        movable = [i for i in range(1, count) if given[i] < largest] or [i for i in range(1, count) if given[i] < bound]
        whole, budget = sum([portions[i] for i in movable]), surplus
        for i in movable:
            extra = min(bound - given[i], max(1, budget * portions[i] // whole), surplus)
            given[i] = given[i] + extra
            surplus = surplus - extra
    return np.array(given)


def normal_values(key, dims, width, most, cuts=(), kind=jnp.bfloat16):
    loudness = block_levels(key, dims, cuts, -0.22, 0.18) if cuts else 1.0
    array = jax.random.normal(key, dims, jnp.float32) * width * loudness
    return jnp.minimum(jnp.maximum(array, -most), most).astype(kind)


def setup_inputs(seed: int = 0) -> dict:
    splits = jax.random.split(jax.random.key(seed), 6)
    inputs = normal_values(splits[0], (TOTAL, D), 1.0, 6.0, ((0, 32),))
    blocks_keys = jax.random.split(jax.random.fold_in(splits[1], 1), TOTAL // ROWS_G)
    blocks_turns = jax.random.permutation(jax.random.fold_in(splits[1], 3), TOTAL // ROWS_G)
    blocks = jax.vmap(lambda own, number: assign_block(jax.random.fold_in(splits[1], 2), own, number, ROWS_G, NB, K, CAP, 2))(blocks_keys, blocks_turns).reshape((TOTAL, K))
    weights = draw_weights(jax.random.fold_in(splits[5], 71), 0)
    enc_bias = normal_values(splits[3], (LATENTS,), 0.5, 3.0, ((0, 8),), jnp.float32)
    dec_bias = normal_values(splits[4], (D,), 0.5, 3.0, (), jnp.float32)
    return dict(inputs=inputs, blocks=blocks, weights=weights, enc_bias=enc_bias, dec_bias=dec_bias)


def reference(inputs, blocks, weights, enc_bias, dec_bias):
    high = lax.Precision.HIGHEST
    w_float = weights.astype(jnp.float32)
    row_norms = jnp.sqrt(lax.optimization_barrier(jnp.sum(w_float * w_float, axis=1)) + 1e-06)
    unit_rows = (w_float / row_norms[:, None]).astype(jnp.bfloat16)
    unit_float = lax.optimization_barrier(unit_rows).astype(jnp.float32)
    latents = LAT_DEV * N_LATENT
    block_total = latents // BLK
    rows_group = ROW_DEV * N_LATENT
    sub_rows = math.gcd(rows_group, 16)
    offsets = jnp.arange(BLK, dtype=jnp.int32)

    def scores_of(group_rows):
        centered_rows = (group_rows.astype(jnp.float32) - dec_bias).astype(jnp.bfloat16)
        full_pre = jnp.dot(unit_rows, centered_rows.T, preferred_element_type=jnp.float32) + enc_bias[:, None]
        return lax.optimization_barrier(jnp.mean(jax.nn.softplus(full_pre).reshape(block_total, BLK, rows_group), axis=1))
    score_groups = lax.map(scores_of, inputs.reshape(N_DP, rows_group, D))
    block_scores = jnp.transpose(score_groups, (1, 0, 2)).reshape(block_total, N_DP * rows_group)

    def rowblock(carry, pieces):
        grad_sums, dot_sums = carry
        row_block, row_lists = pieces
        chosen = (row_lists[:, :, None] * BLK + offsets[None, None, :]).reshape(sub_rows, K * BLK).astype(jnp.int32)
        picked = unit_float[chosen]
        centered = lax.optimization_barrier((row_block.astype(jnp.float32) - dec_bias).astype(jnp.bfloat16)).astype(jnp.float32)
        base_pre = jnp.einsum('rd,rld->rl', centered, picked, precision=high)
        preact = base_pre + enc_bias[chosen]
        latent_codes = lax.optimization_barrier(jax.nn.softplus(preact).astype(jnp.bfloat16)).astype(jnp.float32)
        recon_full = dec_bias + jnp.einsum('rl,rld->rd', latent_codes, picked, precision=high)
        errors = lax.optimization_barrier((recon_full - row_block.astype(jnp.float32)).astype(jnp.bfloat16)).astype(jnp.float32)
        code_grad = jnp.einsum('rd,rld->rl', errors, picked, precision=high)
        pre_grad = lax.optimization_barrier((code_grad * jax.nn.sigmoid(preact)).astype(jnp.bfloat16)).astype(jnp.float32)
        outer_terms = latent_codes[:, :, None] * errors[:, None, :] + pre_grad[:, :, None] * centered[:, None, :]
        flat_ids = chosen.reshape(-1)
        grad_sums = grad_sums.at[flat_ids].add(outer_terms.reshape(-1, D))
        dot_sums = dot_sums.at[flat_ids].add((latent_codes * code_grad + pre_grad * base_pre).reshape(-1))
        return ((grad_sums, dot_sums), recon_full.astype(jnp.bfloat16))

    def group(grad_total, pieces):
        row_block, row_lists = pieces
        zero_carry = (jnp.zeros((latents, D), jnp.float32), jnp.zeros((latents,), jnp.float32))
        (grad_sums, dot_sums), recon_rows = lax.scan(rowblock, zero_carry, (row_block.reshape(-1, sub_rows, D), row_lists.reshape(-1, sub_rows, K)))
        group_part = (grad_sums - unit_float * dot_sums[:, None]) / row_norms[:, None]
        group_part = lax.optimization_barrier(group_part.astype(jnp.bfloat16)).astype(jnp.float32)
        return (grad_total + group_part, recon_rows.reshape(rows_group, D))
    grad_total, recon_rows = lax.scan(group, jnp.zeros((latents, D), jnp.float32), (inputs.reshape(N_DP, rows_group, D), blocks.reshape(N_DP, rows_group, K)))
    return (recon_rows.reshape(-1, D), grad_total, block_scores)
```

```python
import jax
import jax.numpy as jnp
from jax import lax
from jax.sharding import PartitionSpec as P

BLK = 64
CAP = 2
RADIX = 32
LANES = 128
DIRECT = 4


def swap(x, axis, mask):
    size = lax.axis_size(axis)
    return lax.ppermute(x, axis, [(i, i ^ mask) for i in range(size)])


def local(inputs, blocks, weights, enc_bias, dec_bias):
    rows_dev, width = inputs.shape
    lat_rows = weights.shape[0]
    block_count = lat_rows // BLK
    chips = lax.axis_size("latent") // 2
    groups = lax.axis_size("dp")
    half = chips * rows_dev
    rows_group = 2 * half
    col_count = width // groups
    me = lax.axis_index("latent")
    my_group = lax.axis_index("dp")

    lists = jnp.concatenate([blocks // RADIX, blocks % RADIX], axis=1).astype(jnp.bfloat16)
    lists = jnp.pad(lists, ((0, 0), (0, LANES - lists.shape[1])))
    payload = jnp.concatenate([inputs, lists], axis=1)
    both = jnp.concatenate([payload, swap(payload, "latent", 1)], axis=0)
    got = [both] + [swap(both, "latent", 2 * k) for k in range(1, chips)]
    rows = jnp.concatenate([g[:rows_dev] for g in got] + [g[rows_dev:] for g in got], axis=0)

    wide = weights.astype(jnp.float32)
    row_norms = jnp.sqrt(jnp.sum(jnp.square(wide), axis=1) + 1e-06)
    unit_rows = (wide / row_norms[:, None]).astype(jnp.bfloat16)

    group_inputs = rows[:, :width].astype(jnp.float32)
    centered = (group_inputs - dec_bias).astype(jnp.bfloat16)
    top = blocks.shape[1]
    coded = rows[:, width : width + 2 * top].astype(jnp.float32)
    named = (coded[:, :top] * RADIX + coded[:, top:]).astype(jnp.int32)
    block_of = me * block_count + jnp.arange(lat_rows, dtype=jnp.int32) // BLK
    hit = named[:, 0:1] == block_of[None, :]
    for k in range(1, top):
        hit = hit | (named[:, k : k + 1] == block_of[None, :])
    hit = hit.astype(jnp.float32)

    base_pre = lax.dot_general(
        centered, unit_rows, (((1,), (1,)), ((), ())), preferred_element_type=jnp.float32
    )
    preact = base_pre + enc_bias[None, :]
    act = jax.nn.softplus(preact)
    codes = (act * hit).astype(jnp.bfloat16)
    contrib = jnp.dot(codes, unit_rows, preferred_element_type=jnp.float32)
    sums = contrib[:half] + swap(contrib[half:], "latent", 1)
    if chips <= DIRECT:
        parts = [sums] + [swap(sums, "latent", 2 * j) for j in range(1, chips)]
        total = []
        for k in range(chips):
            value = dec_bias
            for j in range(chips):
                at = (k ^ j) * rows_dev
                value = value + parts[j][at : at + rows_dev]
            total.append(value)
        recon_full = jnp.concatenate(total, axis=0)
        errors = (recon_full - group_inputs[:half]).astype(jnp.bfloat16)
    else:
        recon_full = dec_bias + sums[:rows_dev]
        for j in range(1, chips):
            recon_full = recon_full + swap(sums[j * rows_dev : (j + 1) * rows_dev], "latent", 2 * j)
        errors = (recon_full - group_inputs[:rows_dev]).astype(jnp.bfloat16)
        errors = [errors] + [swap(errors, "latent", 2 * j) for j in range(1, chips)]
        errors = jnp.concatenate(errors, axis=0)
    recon_rows = recon_full[:rows_dev].astype(jnp.bfloat16)
    errors = jnp.concatenate([errors, swap(errors, "latent", 1)], axis=0)

    means = jnp.mean(act.reshape(rows_group, block_count, BLK), axis=2)
    place = jnp.arange(rows_group, dtype=jnp.int32)
    owner = (place // rows_dev) ^ me
    relative = (owner % 2) * half + (owner // 2) * rows_dev + place % rows_dev
    order = (relative[None, :] == place[:, None]).astype(jnp.float32)
    block_scores = lax.dot_general(
        means, order, (((0,), (0,)), ((), ())), precision=lax.Precision.HIGHEST
    )

    code_grad = lax.dot_general(
        errors, unit_rows, (((1,), (1,)), ((), ())), preferred_element_type=jnp.float32
    )
    pre_grad = (code_grad * jax.nn.sigmoid(preact) * hit).astype(jnp.bfloat16)
    along = jnp.sum(
        codes.astype(jnp.float32) * code_grad + pre_grad.astype(jnp.float32) * base_pre, axis=0
    )
    along_high = lax.reduce_precision(along, 8, 7)
    along_low = along - along_high

    earlier = (place[:, None] > place[None, :]).astype(jnp.float32)
    before = jnp.dot(earlier, hit)
    compact = []
    for s in range(CAP):
        mine = hit * (before == s)
        compact.append(jnp.sum(mine * codes.astype(jnp.float32), axis=0))
        compact.append(jnp.sum(mine * pre_grad.astype(jnp.float32), axis=0))
        compact.append(jnp.sum(mine * (place[:, None] + 1).astype(jnp.float32), axis=0))
    compact = jnp.stack(compact + [along_high, along_low]).astype(jnp.bfloat16)
    right = jnp.concatenate([errors, centered], axis=0)
    flat = compact.reshape(-1, col_count)
    sent = []
    for k in range(groups):
        cols = lax.dynamic_slice_in_dim(right, (my_group ^ k) * col_count, col_count, 1)
        packet = jnp.concatenate([cols, flat], axis=0)
        sent.append(swap(packet, "dp", k) if k else packet)

    lefts, rights, alongs = [], [], []
    for packet in sent:
        rights.append(packet[: 2 * rows_group])
        terms = packet[2 * rows_group :].reshape(-1, lat_rows).astype(jnp.float32)
        code_part, grad_part = 0.0, 0.0
        for s in range(CAP):
            at = (terms[3 * s + 2][None, :] == (place[:, None] + 1).astype(jnp.float32)).astype(
                jnp.float32
            )
            code_part = code_part + at * terms[3 * s][None, :]
            grad_part = grad_part + at * terms[3 * s + 1][None, :]
        lefts += [code_part, grad_part]
        alongs.append(terms[3 * CAP] + terms[3 * CAP + 1])
    outer = 0.0
    for g in range(0, groups, DIRECT):
        left = jnp.concatenate(lefts[2 * g : 2 * (g + DIRECT)], axis=0).astype(jnp.bfloat16)
        right = jnp.concatenate(rights[g : g + DIRECT], axis=0)
        outer = outer + lax.dot_general(
            left, right, (((0,), (0,)), ((), ())), preferred_element_type=jnp.float32
        )
    along_all = sum(alongs)
    unit_cols = lax.dynamic_slice_in_dim(unit_rows, my_group * col_count, col_count, 1)
    grad_weights = (outer - unit_cols.astype(jnp.float32) * along_all[:, None]) / row_norms[:, None]
    return (recon_rows, grad_weights, block_scores)


def solution(mesh):
    in_specs = (
        P(("dp", "latent"), None),
        P(("dp", "latent"), None),
        P("latent", None),
        P("latent"),
        P(),
    )
    out_specs = (P(("dp", "latent"), None), P("latent", "dp"), P("latent", "dp"))
    return jax.shard_map(local, mesh=mesh, in_specs=in_specs, out_specs=out_specs, check_vma=False)
```

```python
import functools

import jax
import jax.numpy as jnp
from jax import lax
from jax.experimental import pallas as pl
from jax.experimental.pallas import tpu as pltpu
from jax.sharding import PartitionSpec as P

BLK = 64
CAP = 2
RADIX = 32
LANES = 128
DIRECT = 4
TERMS = 8
VMEM = pl.BlockSpec(memory_space=pltpu.VMEM)
HBM = pl.BlockSpec(memory_space=pltpu.MemorySpace.HBM)
ANY = pl.BlockSpec(memory_space=pl.ANY)
F32, BF16 = jnp.float32, jnp.bfloat16


def swap(x, axis, mask):
    size = lax.axis_size(axis)
    return lax.ppermute(x, axis, [(i, i ^ mask) for i in range(size)])


def params(mib):
    return pltpu.CompilerParams(vmem_limit_bytes=mib * 2**20)


def shape(dims, dtype):
    return jax.ShapeDtypeStruct(dims, dtype)


def normalize_kernel(after_ref, weights_ref, unit_ref, turned_ref, norms_ref, held_ref, sems):
    del after_ref
    lat_rows, width = weights_ref.shape
    copies = []
    for at in range(lat_rows // LANES):
        rows = pl.ds(at * LANES, LANES)
        copies.append(
            pltpu.make_async_copy(weights_ref.at[rows], held_ref.at[rows], sems.at[at])
        )
        copies[-1].start()
    for at, copy in enumerate(copies):
        copy.wait()
        rows = pl.ds(at * LANES, LANES)
        squares = jnp.zeros((LANES, LANES), F32)
        for left in range(0, width, LANES):
            tile = held_ref[rows, left : left + LANES].astype(F32)
            squares = squares + tile * tile
        norms = jnp.sqrt(jnp.sum(squares, axis=1, keepdims=True) + 1e-06)
        norms_ref[rows, :] = norms
        scale = jnp.broadcast_to(1.0 / norms, (LANES, LANES))
        for left in range(0, width, LANES):
            tile = held_ref[rows, left : left + LANES].astype(F32)
            unit = (tile * scale).astype(BF16)
            unit_ref[rows, left : left + LANES] = unit
            turned_ref[left : left + LANES, rows] = unit.T


def normalize(after, weights):
    lat_rows, width = weights.shape
    return pl.pallas_call(
        normalize_kernel,
        name="normalize",
        out_shape=(
            shape((lat_rows, width), BF16),
            shape((width, lat_rows), BF16),
            shape((lat_rows, 1), F32),
        ),
        in_specs=[ANY, HBM],
        out_specs=(VMEM, VMEM, VMEM),
        scratch_shapes=[
            pltpu.VMEM((lat_rows, width), BF16),
            pltpu.SemaphoreType.DMA((lat_rows // LANES,)),
        ],
        compiler_params=params(20),
        cost_estimate=pl.CostEstimate(
            flops=4 * lat_rows * width, bytes_accessed=6 * lat_rows * width, transcendentals=0
        ),
    )(after, weights)


def forward_kernel(rows_dev, top, dec_ref, enc_ref, unit_ref, turned_ref, *refs):
    chips = len(refs) - 9
    pieces = refs[:chips]
    keep_ref, send_ref, cent_ref, own_ref, codes_ref, base_ref, act_ref, hit_ref, rows_ref = refs[
        chips:
    ]
    half = chips * rows_dev
    lat_rows, width = unit_ref.shape
    for k, piece in enumerate(pieces):
        value = piece[...].astype(F32)
        rows_ref[k * rows_dev : (k + 1) * rows_dev, :] = value[:rows_dev]
        rows_ref[half + k * rows_dev : half + (k + 1) * rows_dev, :] = value[rows_dev:]
    own_ref[...] = rows_ref[:half, :width]
    centered = (rows_ref[:, :width] - dec_ref[...]).astype(BF16)
    cent_ref[...] = centered
    base = jnp.dot(centered, turned_ref[...], preferred_element_type=F32)
    base_ref[...] = base
    preact = base + enc_ref[...]
    act = jnp.maximum(preact, 0.0) + jnp.log1p(jnp.exp(-jnp.abs(preact)))
    act_ref[...] = act
    first = lax.axis_index("latent") * (lat_rows // BLK)
    lat = lax.broadcasted_iota(jnp.int32, (2 * half, lat_rows), 1)
    block_of = (first + lat // BLK).astype(F32)
    names = rows_ref[:, width:]
    hit = jnp.zeros((2 * half, lat_rows), F32)
    for k in range(top):
        name = names[:, k : k + 1] * RADIX + names[:, top + k : top + k + 1]
        hit = jnp.where(name == block_of, 1.0, hit)
    hit_ref[...] = hit
    codes = (act * hit).astype(BF16)
    codes_ref[...] = codes
    contrib = jnp.dot(codes, unit_ref[...], preferred_element_type=F32)
    keep_ref[...] = contrib[:half]
    send_ref[...] = contrib[half:]


def forward(rows_dev, top, dec, enc, unit, turned, pieces):
    lat_rows, width = unit.shape
    half = len(pieces) * rows_dev
    count = 2 * half
    return pl.pallas_call(
        functools.partial(forward_kernel, rows_dev, top),
        name="forward",
        out_shape=(
            shape((half, width), F32),
            shape((half, width), F32),
            shape((count, width), BF16),
            shape((half, width), F32),
            shape((count, lat_rows), BF16),
            shape((count, lat_rows), F32),
            shape((count, lat_rows), F32),
            shape((count, lat_rows), F32),
        ),
        in_specs=[VMEM] * (4 + len(pieces)),
        out_specs=(VMEM,) * 8,
        scratch_shapes=[pltpu.VMEM((count, width + LANES), F32)],
        compiler_params=params(20),
        cost_estimate=pl.CostEstimate(
            flops=4 * count * lat_rows * width,
            bytes_accessed=4 * lat_rows * width,
            transcendentals=2 * count * lat_rows,
        ),
    )(dec, enc, unit, turned, *pieces)


def side_kernel(rows_dev, act_ref, hit_ref, codes_ref, base_ref, enc_ref, *outs):
    scores_ref, gate_ref, second_ref, compact_ref = outs
    count, lat_rows = act_ref.shape
    block_count = lat_rows // BLK
    half = count // 2
    me = lax.axis_index("latent")
    latent = lax.broadcasted_iota(jnp.int32, (block_count, lat_rows), 1)
    block = lax.broadcasted_iota(jnp.int32, (block_count, lat_rows), 0)
    inside = jnp.where(latent // BLK == block, 1.0 / BLK, 0.0).astype(F32)
    means = lax.dot_general(
        inside,
        act_ref[...],
        (((1,), (1,)), ((), ())),
        preferred_element_type=F32,
        precision=lax.Precision.HIGHEST,
    )
    at = lax.broadcasted_iota(jnp.int32, (count, count), 0)
    place = lax.broadcasted_iota(jnp.int32, (count, count), 1)
    owner = (place // rows_dev) ^ me
    relative = (owner % 2) * half + (owner // 2) * rows_dev + place % rows_dev
    order = jnp.where(relative == at, 1.0, 0.0).astype(F32)
    scores_ref[...] = jnp.dot(
        means, order, preferred_element_type=F32, precision=lax.Precision.HIGHEST
    )
    hit = hit_ref[...]
    preact = base_ref[...] + enc_ref[...]
    gate_ref[...] = hit * jax.nn.sigmoid(preact)
    earlier = jnp.where(place < at, 1.0, 0.0).astype(BF16)
    before = jnp.dot(earlier, hit.astype(BF16), preferred_element_type=F32)
    second = jnp.where(before == 1.0, hit, 0.0)
    first = jnp.where(before == 0.0, hit, 0.0)
    second_ref[...] = second
    codes = codes_ref[...].astype(F32)
    number = (lax.broadcasted_iota(jnp.int32, (count, lat_rows), 0) + 1).astype(F32)
    rows = []
    for slot in (first, second):
        rows.append(jnp.sum(slot * codes, axis=0, keepdims=True))
    for slot in (first, second):
        rows.append(jnp.sum(slot * number, axis=0, keepdims=True))
    for at, row in enumerate(rows):
        compact_ref[at : at + 1, :] = row


def side(rows_dev, act, hit, codes, base, enc):
    count, lat_rows = act.shape
    return pl.pallas_call(
        functools.partial(side_kernel, rows_dev),
        name="side",
        out_shape=(
            shape((lat_rows // BLK, count), F32),
            shape((count, lat_rows), F32),
            shape((count, lat_rows), F32),
            shape((2 * CAP, lat_rows), F32),
        ),
        in_specs=[VMEM] * 5,
        out_specs=(VMEM,) * 4,
        compiler_params=params(20),
        cost_estimate=pl.CostEstimate(
            flops=8 * count * lat_rows * 64, bytes_accessed=32 * count * lat_rows, transcendentals=0
        ),
    )(act, hit, codes, base, enc)


def errors_kernel(rows_dev, dec_ref, own_ref, *refs):
    parts, (recon_ref, errors_ref) = refs[:-2], refs[-2:]
    chips = len(parts)
    total = parts[0][...]
    for j in range(1, chips):
        value = parts[j][...]
        turned = [
            value[(k ^ j) * rows_dev : ((k ^ j) + 1) * rows_dev] for k in range(chips)
        ]
        total = total + jnp.concatenate(turned, axis=0)
    full = total + dec_ref[...]
    recon_ref[...] = full[:rows_dev].astype(BF16)
    errors_ref[...] = (full - own_ref[...]).astype(BF16)


def errors_of(rows_dev, dec, own, parts):
    half, width = own.shape
    return pl.pallas_call(
        functools.partial(errors_kernel, rows_dev),
        name="errors",
        out_shape=(shape((rows_dev, width), BF16), shape((half, width), BF16)),
        in_specs=[VMEM] * (2 + len(parts)),
        out_specs=(VMEM, VMEM),
        compiler_params=params(16),
    )(dec, own, *parts)


def backward_kernel(groups, turned_ref, mine_ref, other_ref, cent_ref, *refs):
    codes_ref, base_ref, gate_ref, second_ref, compact_ref = refs[:5]
    packets, errors_ref = refs[5:-1], refs[-1]
    width, lat_rows = turned_ref.shape
    half = mine_ref.shape[0]
    count = 2 * half
    cols = width // groups
    errors_ref[:half, :] = mine_ref[...]
    errors_ref[half:, :] = other_ref[...]
    grad = jnp.dot(errors_ref[...], turned_ref[...], preferred_element_type=F32)
    pre_grad = (grad * gate_ref[...]).astype(BF16).astype(F32)
    codes = codes_ref[...].astype(F32)
    along = jnp.sum(codes * grad + pre_grad * base_ref[...], axis=0, keepdims=True)
    high = along.astype(BF16).astype(F32)
    both = jnp.sum(pre_grad, axis=0, keepdims=True)
    later = jnp.sum(pre_grad * second_ref[...], axis=0, keepdims=True)
    table = compact_ref[...]
    terms = jnp.concatenate([table, both - later, later, high, along - high], axis=0).astype(BF16)
    group = lax.axis_index("dp")
    for k, packet in enumerate(packets):
        at = pl.ds(pl.multiple_of((group ^ k) * cols, LANES), cols)
        packet[:count, :] = errors_ref[:, at]
        packet[count : 2 * count, :] = cent_ref[:, at]
        for part in range(lat_rows // cols):
            rows = pl.ds(2 * count + part * TERMS, TERMS)
            packet[rows, :] = terms[:, part * cols : (part + 1) * cols]


def backward(groups, turned, mine, other, cent, codes, base, gate, second, compact):
    width, lat_rows = turned.shape
    count = cent.shape[0]
    cols = width // groups
    packet = shape((2 * count + TERMS * lat_rows // cols, cols), BF16)
    return pl.pallas_call(
        functools.partial(backward_kernel, groups),
        name="backward",
        out_shape=(packet,) * groups,
        in_specs=[VMEM] * 9,
        out_specs=(VMEM,) * groups,
        scratch_shapes=[pltpu.VMEM((count, width), BF16)],
        compiler_params=params(20),
        cost_estimate=pl.CostEstimate(
            flops=2 * count * lat_rows * width, bytes_accessed=2 * lat_rows * width, transcendentals=0
        ),
    )(turned, mine, other, cent, codes, base, gate, second, compact)


def gradient_kernel(count, unit_ref, norms_ref, *refs):
    out_ref, left_ref, right_ref, held_ref, sems = refs[-5:]
    packets = refs[:-5]
    lat_rows, cols = out_ref.shape
    along = jnp.zeros((1, lat_rows), F32)
    number = (lax.broadcasted_iota(jnp.int32, (count, lat_rows), 0) + 1).astype(F32)
    for g, packet in enumerate(packets):
        base = g * 2 * count
        right_ref[base : base + 2 * count, :] = packet[: 2 * count, :]
        parts = [
            packet[2 * count + p * TERMS : 2 * count + (p + 1) * TERMS, :].astype(F32)
            for p in range(lat_rows // cols)
        ]
        terms = jnp.concatenate(parts, axis=1)
        code0, code1, row0, row1, grad0, grad1, high, low = [
            terms[t : t + 1] for t in range(TERMS)
        ]
        at0, at1 = number == row0, number == row1
        code = jnp.where(at0, code0, jnp.where(at1, code1, 0.0))
        grad = jnp.where(at0, grad0, jnp.where(at1, grad1, 0.0))
        left_ref[base : base + count, :] = code.astype(BF16)
        left_ref[base + count : base + 2 * count, :] = grad.astype(BF16)
        along = along + (high + low)
    start = pl.multiple_of(lax.axis_index("dp") * cols, LANES)
    copies = []
    for at in range(lat_rows // LANES):
        rows = pl.ds(at * LANES, LANES)
        outer = lax.dot_general(
            left_ref[:, rows],
            right_ref[...],
            (((0,), (0,)), ((), ())),
            preferred_element_type=F32,
        )
        column = jnp.broadcast_to(along[:, at * LANES : (at + 1) * LANES], (LANES, LANES)).T
        unit = unit_ref[rows, pl.ds(start, cols)].astype(F32)
        inverse = 1.0 / norms_ref[rows, :]
        held_ref[rows, :] = (outer - unit * column[:, :1]) * inverse
        copies.append(pltpu.make_async_copy(held_ref.at[rows], out_ref.at[rows], sems.at[at]))
        copies[-1].start()
    for copy in copies:
        copy.wait()


def gradient(count, unit, norms, packets):
    lat_rows = unit.shape[0]
    cols = packets[0].shape[1]
    depth = 2 * count * len(packets)
    return pl.pallas_call(
        functools.partial(gradient_kernel, count),
        name="gradient",
        out_shape=shape((lat_rows, cols), F32),
        in_specs=[VMEM] * (2 + len(packets)),
        out_specs=HBM,
        scratch_shapes=[
            pltpu.VMEM((depth, lat_rows), BF16),
            pltpu.VMEM((depth, cols), BF16),
            pltpu.VMEM((lat_rows, cols), F32),
            pltpu.SemaphoreType.DMA((lat_rows // LANES,)),
        ],
        compiler_params=params(24),
        cost_estimate=pl.CostEstimate(
            flops=2 * depth * lat_rows * cols, bytes_accessed=8 * lat_rows * cols, transcendentals=0
        ),
    )(unit, norms, *packets)


def local(inputs, blocks, weights, enc_bias, dec_bias):
    rows_dev = inputs.shape[0]
    top = blocks.shape[1]
    chips = lax.axis_size("latent") // 2
    groups = lax.axis_size("dp")
    count = 2 * chips * rows_dev
    dec, enc = dec_bias[None, :], enc_bias[None, :]

    both_rows = jnp.concatenate([inputs, swap(inputs, "latent", 1)], axis=0)
    both_names = jnp.concatenate([blocks, swap(blocks, "latent", 1)], axis=0)
    lists = jnp.concatenate([both_names // RADIX, both_names % RADIX], axis=1).astype(BF16)
    lists = jnp.pad(lists, ((0, 0), (0, LANES - lists.shape[1])))
    both = jnp.concatenate([both_rows, lists], axis=1)
    pieces = [both] + [swap(both, "latent", 2 * k) for k in range(1, chips)]

    unit, turned, norms = normalize(both, weights)
    keep, send, cent, own, codes, base, act, hit = forward(
        rows_dev, top, dec, enc, unit, turned, pieces
    )
    sums = keep + swap(send, "latent", 1)
    if chips <= DIRECT:
        parts = [sums] + [swap(sums, "latent", 2 * j) for j in range(1, chips)]
        recon, errors = errors_of(rows_dev, dec, own, parts)
    else:
        full = dec_bias + sums[:rows_dev]
        for j in range(1, chips):
            full = full + swap(sums[j * rows_dev : (j + 1) * rows_dev], "latent", 2 * j)
        recon = full.astype(BF16)
        errors = (full - own[:rows_dev]).astype(BF16)
        errors = [errors] + [swap(errors, "latent", 2 * j) for j in range(1, chips)]
        errors = jnp.concatenate(errors, axis=0)
    block_scores, gate, second, compact = side(rows_dev, act, hit, codes, base, enc)
    other = swap(errors, "latent", 1)
    packets = backward(
        groups, turned, errors, other, cent, codes, base, gate, second, compact
    )
    packets = [swap(p, "dp", k) if k else p for k, p in enumerate(packets)]
    grad_weights = gradient(count, unit, norms, packets)
    return (recon, grad_weights, block_scores)


def solution(mesh):
    in_specs = (
        P(("dp", "latent"), None),
        P(("dp", "latent"), None),
        P("latent", None),
        P("latent"),
        P(),
    )
    out_specs = (P(("dp", "latent"), None), P("latent", "dp"), P("latent", "dp"))
    return jax.shard_map(local, mesh=mesh, in_specs=in_specs, out_specs=out_specs, check_vma=False)
```

```python
import functools

import jax
import jax.numpy as jnp
from jax import lax
from jax.experimental import pallas as pl
from jax.experimental.pallas import tpu as pltpu
from jax.sharding import PartitionSpec as P

BLK = 64
CAP = 2
RADIX = 32
LANES = 128
DIRECT = 4
TERMS = 8
HEAD = 256
VMEM = pl.BlockSpec(memory_space=pltpu.VMEM)
HBM = pl.BlockSpec(memory_space=pltpu.MemorySpace.HBM)
ANY = pl.BlockSpec(memory_space=pl.ANY)
F32, BF16 = jnp.float32, jnp.bfloat16


def swap(x, axis, mask):
    size = lax.axis_size(axis)
    return lax.ppermute(x, axis, [(i, i ^ mask) for i in range(size)])


def params(mib):
    return pltpu.CompilerParams(vmem_limit_bytes=mib * 2**20)


def shape(dims, dtype):
    return jax.ShapeDtypeStruct(dims, dtype)


def pack_kernel(own_ref, mate_ref, names_ref, mate_names_ref, out_ref):
    rows_dev, width = own_ref.shape
    out_ref[:rows_dev, :width] = own_ref[...]
    out_ref[rows_dev:, :width] = mate_ref[...]
    lane = lax.broadcasted_iota(jnp.int32, (rows_dev, LANES), 1)
    for at, ref in enumerate((names_ref, mate_names_ref)):
        names = ref[...]
        top = names.shape[1]
        coded = jnp.zeros((rows_dev, LANES), jnp.int32)
        for k in range(top):
            name = names[:, k : k + 1]
            coded = jnp.where(lane == k, name // RADIX, coded)
            coded = jnp.where(lane == top + k, name % RADIX, coded)
        out_ref[at * rows_dev : (at + 1) * rows_dev, width:] = coded.astype(F32).astype(BF16)


def pack(own, mate, names, mate_names):
    rows_dev, width = own.shape
    return pl.pallas_call(
        pack_kernel,
        name="pack",
        out_shape=shape((2 * rows_dev, width + LANES), BF16),
        in_specs=[VMEM] * 4,
        out_specs=VMEM,
        compiler_params=params(4),
    )(own, mate, names, mate_names)


def normalize_kernel(first_row, *refs):
    weights_ref, extra = refs[0], refs[1:3]
    unit_ref, turned_ref, norms_ref = refs[3:6]
    held_ref, sems = refs[-2:]
    lat_rows, width = unit_ref.shape
    copies = []
    for at in range(lat_rows // LANES):
        rows = pl.ds(at * LANES, LANES)
        source = weights_ref.at[pl.ds(first_row + at * LANES, LANES)]
        copies.append(pltpu.make_async_copy(source, held_ref.at[rows], sems.at[at]))
        copies[-1].start()
    for ref, out in zip(extra, refs[6:-2]):
        copies.append(pltpu.make_async_copy(ref, out, sems.at[len(copies)]))
        copies[-1].start()
    for at in range(lat_rows // LANES):
        copies[at].wait()
        rows = pl.ds(at * LANES, LANES)
        squares = jnp.zeros((LANES, LANES), F32)
        for left in range(0, width, LANES):
            tile = held_ref[rows, left : left + LANES].astype(F32)
            squares = squares + tile * tile
        norms = jnp.sqrt(jnp.sum(squares, axis=1, keepdims=True) + 1e-06)
        norms_ref[rows, :] = norms
        scale = jnp.broadcast_to(1.0 / norms, (LANES, LANES))
        for left in range(0, width, LANES):
            tile = held_ref[rows, left : left + LANES].astype(F32)
            unit = (tile * scale).astype(BF16)
            unit_ref[rows, left : left + LANES] = unit
            turned_ref[left : left + LANES, rows] = unit.T
    for copy in copies[lat_rows // LANES :]:
        copy.wait()


def normalize(name, weights, first_row, lat_rows, extra, brought, mib):
    width = weights.shape[1]
    outs = (
        shape((lat_rows, width), BF16),
        shape((width, lat_rows), BF16),
        shape((lat_rows, 1), F32),
    )
    if brought:
        outs += tuple(shape(x.shape, x.dtype) for x in extra)
    return pl.pallas_call(
        functools.partial(normalize_kernel, first_row),
        name=name,
        out_shape=outs,
        in_specs=[HBM, ANY, ANY],
        out_specs=(VMEM,) * len(outs),
        scratch_shapes=[
            pltpu.VMEM((lat_rows, width), BF16),
            pltpu.SemaphoreType.DMA((lat_rows // LANES + 2,)),
        ],
        compiler_params=params(mib),
        cost_estimate=pl.CostEstimate(
            flops=4 * lat_rows * width, bytes_accessed=6 * lat_rows * width, transcendentals=0
        ),
    )(weights, *extra)


def forward_kernel(rows_dev, top, splits, dec_ref, enc_ref, *refs):
    units, turneds, refs = refs[:splits], refs[splits : 2 * splits], refs[2 * splits :]
    chips = len(refs) - 8
    pieces = refs[:chips]
    contrib_ref, cent_ref, input_ref, codes_ref, base_ref, act_ref, hit_ref, rows_ref = refs[chips:]
    half = chips * rows_dev
    width, lat_rows = units[0].shape[1], base_ref.shape[1]
    for k, piece in enumerate(pieces):
        value = piece[...].astype(F32)
        rows_ref[k * rows_dev : (k + 1) * rows_dev, :] = value[:rows_dev]
        rows_ref[half + k * rows_dev : half + (k + 1) * rows_dev, :] = value[rows_dev:]
    input_ref[...] = rows_ref[:, :width].astype(BF16)
    centered = (rows_ref[:, :width] - dec_ref[...]).astype(BF16)
    cent_ref[...] = centered
    base = times(centered, turneds)
    base_ref[...] = base
    preact = base + enc_ref[...]
    act = jnp.maximum(preact, 0.0) + jnp.log1p(jnp.exp(-jnp.abs(preact)))
    act_ref[...] = act
    first = lax.axis_index("latent") * (lat_rows // BLK)
    lat = lax.broadcasted_iota(jnp.int32, (2 * half, lat_rows), 1)
    block_of = (first + lat // BLK).astype(F32)
    names = rows_ref[:, width:]
    hit = jnp.zeros((2 * half, lat_rows), F32)
    for k in range(top):
        name = names[:, k : k + 1] * RADIX + names[:, top + k : top + k + 1]
        hit = jnp.where(name == block_of, 1.0, hit)
    hit_ref[...] = hit
    codes = (act * hit).astype(BF16)
    codes_ref[...] = codes
    at, contrib = 0, None
    for unit in units:
        part = codes[:, at : at + unit.shape[0]]
        term = jnp.dot(part, unit[...], preferred_element_type=F32)
        contrib = term if contrib is None else contrib + term
        at += unit.shape[0]
    contrib_ref[...] = contrib


def times(x, parts):
    return jnp.concatenate(
        [jnp.dot(x, part[...], preferred_element_type=F32) for part in parts], axis=1
    )


def forward(rows_dev, top, dec, enc, units, turneds, pieces):
    lat_rows, width = enc.shape[1], units[0].shape[1]
    count = 2 * len(pieces) * rows_dev
    return pl.pallas_call(
        functools.partial(forward_kernel, rows_dev, top, len(units)),
        name="forward",
        out_shape=(
            shape((count, width), F32),
            shape((count, width), BF16),
            shape((count, width), BF16),
            shape((count, lat_rows), BF16),
            shape((count, lat_rows), F32),
            shape((count, lat_rows), F32),
            shape((count, lat_rows), F32),
        ),
        in_specs=[VMEM] * (2 + 2 * len(units) + len(pieces)),
        out_specs=(VMEM,) * 7,
        scratch_shapes=[pltpu.VMEM((count, width + LANES), F32)],
        compiler_params=params(20),
        cost_estimate=pl.CostEstimate(
            flops=4 * count * lat_rows * width,
            bytes_accessed=4 * lat_rows * width,
            transcendentals=2 * count * lat_rows,
        ),
    )(dec, enc, *units, *turneds, *pieces)


def side_kernel(rows_dev, act_ref, hit_ref, codes_ref, base_ref, enc_ref, *outs):
    scores_ref, gate_ref, second_ref, compact_ref = outs
    count, lat_rows = act_ref.shape
    block_count = lat_rows // BLK
    half = count // 2
    me = lax.axis_index("latent")
    latent = lax.broadcasted_iota(jnp.int32, (block_count, lat_rows), 1)
    block = lax.broadcasted_iota(jnp.int32, (block_count, lat_rows), 0)
    inside = jnp.where(latent // BLK == block, 1.0 / BLK, 0.0).astype(F32)
    means = lax.dot_general(
        inside,
        act_ref[...],
        (((1,), (1,)), ((), ())),
        preferred_element_type=F32,
        precision=lax.Precision.HIGHEST,
    )
    at = lax.broadcasted_iota(jnp.int32, (count, count), 0)
    place = lax.broadcasted_iota(jnp.int32, (count, count), 1)
    owner = (place // rows_dev) ^ me
    relative = (owner % 2) * half + (owner // 2) * rows_dev + place % rows_dev
    order = jnp.where(relative == at, 1.0, 0.0).astype(F32)
    scores_ref[...] = jnp.dot(
        means, order, preferred_element_type=F32, precision=lax.Precision.HIGHEST
    )
    hit = hit_ref[...]
    preact = base_ref[...] + enc_ref[...]
    gate_ref[...] = hit * jax.nn.sigmoid(preact)
    earlier = jnp.where(place < at, 1.0, 0.0).astype(BF16)
    before = jnp.dot(earlier, hit.astype(BF16), preferred_element_type=F32)
    second = jnp.where(before == 1.0, hit, 0.0)
    first = jnp.where(before == 0.0, hit, 0.0)
    second_ref[...] = second
    codes = codes_ref[...].astype(F32)
    number = (lax.broadcasted_iota(jnp.int32, (count, lat_rows), 0) + 1).astype(F32)
    rows = []
    for slot in (first, second):
        rows.append(jnp.sum(slot * codes, axis=0, keepdims=True))
    for slot in (first, second):
        rows.append(jnp.sum(slot * number, axis=0, keepdims=True))
    for at, row in enumerate(rows):
        compact_ref[at : at + 1, :] = row


def side(rows_dev, act, hit, codes, base, enc):
    count, lat_rows = act.shape
    return pl.pallas_call(
        functools.partial(side_kernel, rows_dev),
        name="side",
        out_shape=(
            shape((lat_rows // BLK, count), F32),
            shape((count, lat_rows), F32),
            shape((count, lat_rows), F32),
            shape((2 * CAP, lat_rows), F32),
        ),
        in_specs=[VMEM] * 5,
        out_specs=(VMEM,) * 4,
        compiler_params=params(20),
        cost_estimate=pl.CostEstimate(
            flops=8 * count * lat_rows * 64, bytes_accessed=32 * count * lat_rows, transcendentals=0
        ),
    )(act, hit, codes, base, enc)


def combine_kernel(mine_ref, mate_ref, sums_ref, sent_ref):
    half = mine_ref.shape[0] // 2
    for at, other in ((0, half), (half, 0)):
        sums = mine_ref[at : at + half, :] + mate_ref[other : other + half, :]
        sums_ref[at : at + half, :] = sums
        sent_ref[at : at + half, :] = sums.astype(BF16)


def combine(mine, mate):
    return pl.pallas_call(
        combine_kernel,
        name="combine",
        out_shape=(shape(mine.shape, F32), shape(mine.shape, BF16)),
        in_specs=[VMEM] * 2,
        out_specs=(VMEM, VMEM),
        compiler_params=params(12),
    )(mine, mate)


def errors_kernel(rows_dev, dec_ref, input_ref, sums_ref, parts, recon_ref, errors_ref):
    chips = len(parts) + 1
    total = sums_ref[...]
    for j, part in enumerate(parts, 1):
        value = part[...].astype(F32)
        turned = []
        for k in range(2 * chips):
            at = (k ^ j) * rows_dev
            turned.append(value[at : at + rows_dev])
        total = total + jnp.concatenate(turned, axis=0)
    full = total + dec_ref[...]
    recon_ref[...] = full[:rows_dev].astype(BF16)
    errors_ref[...] = (full - input_ref[...].astype(F32)).astype(BF16)


def backward_kernel(groups, rows_dev, splits, *refs):
    turneds, refs = refs[:splits], refs[splits:]
    cent_ref, codes_ref, base_ref, gate_ref = refs[:4]
    refs = refs[4:]
    second_ref, compact_ref = refs[:2]
    if rows_dev:
        chips = cent_ref.shape[0] // (2 * rows_dev)
        dec_ref, input_ref, sums_ref = refs[2:5]
        parts, outs = refs[5 : 4 + chips], refs[4 + chips :]
        recon_ref, packets, errors_ref = outs[0], outs[1:-1], outs[-1]
        errors_kernel(rows_dev, dec_ref, input_ref, sums_ref, parts, recon_ref, errors_ref)
    else:
        errors_ref, packets = refs[2], refs[3:]
    count, width = cent_ref.shape
    lat_rows = codes_ref.shape[1]
    cols = width // groups
    grad = times(errors_ref[...], turneds)
    pre_grad = (grad * gate_ref[...]).astype(BF16).astype(F32)
    codes = codes_ref[...].astype(F32)
    along = jnp.sum(codes * grad + pre_grad * base_ref[...], axis=0, keepdims=True)
    high = along.astype(BF16).astype(F32)
    both = jnp.sum(pre_grad, axis=0, keepdims=True)
    later = jnp.sum(pre_grad * second_ref[...], axis=0, keepdims=True)
    table = compact_ref[...]
    terms = jnp.concatenate([table, both - later, later, high, along - high], axis=0).astype(BF16)
    group = lax.axis_index("dp")
    for k, packet in enumerate(packets):
        at = pl.ds(pl.multiple_of((group ^ k) * cols, LANES), cols)
        packet[:count, :] = errors_ref[:, at]
        packet[count : 2 * count, :] = cent_ref[:, at]
        for part in range(lat_rows // cols):
            rows = pl.ds(2 * count + part * TERMS, TERMS)
            packet[rows, :] = terms[:, part * cols : (part + 1) * cols]


def backward(groups, rows_dev, turneds, cent, rest):
    count, width = cent.shape
    lat_rows = rest[0].shape[1]
    cols = width // groups
    packet = shape((2 * count + TERMS * lat_rows // cols, cols), BF16)
    outs = (packet,) * groups
    scratch = []
    if rows_dev:
        outs = (shape((rows_dev, width), BF16),) + outs
        scratch = [pltpu.VMEM((count, width), BF16)]
    return pl.pallas_call(
        functools.partial(backward_kernel, groups, rows_dev, len(turneds)),
        name="backward",
        out_shape=outs,
        in_specs=[VMEM] * (len(turneds) + 1 + len(rest)),
        out_specs=(VMEM,) * len(outs),
        scratch_shapes=scratch,
        compiler_params=params(20),
        cost_estimate=pl.CostEstimate(
            flops=2 * count * lat_rows * width, bytes_accessed=2 * lat_rows * width, transcendentals=0
        ),
    )(*turneds, cent, *rest)


def gradient_kernel(count, splits, *refs):
    units, norms, refs = refs[:splits], refs[splits : 2 * splits], refs[2 * splits :]
    out_ref, left_ref, right_ref, held_ref, sems = refs[-5:]
    packets = refs[:-5]
    lat_rows, cols = out_ref.shape
    along = jnp.zeros((1, lat_rows), F32)
    number = (lax.broadcasted_iota(jnp.int32, (count, lat_rows), 0) + 1).astype(F32)
    for g, packet in enumerate(packets):
        base = g * 2 * count
        right_ref[base : base + 2 * count, :] = packet[: 2 * count, :]
        parts = [
            packet[2 * count + p * TERMS : 2 * count + (p + 1) * TERMS, :].astype(F32)
            for p in range(lat_rows // cols)
        ]
        terms = jnp.concatenate(parts, axis=1)
        code0, code1, row0, row1, grad0, grad1, high, low = [
            terms[t : t + 1] for t in range(TERMS)
        ]
        at0, at1 = number == row0, number == row1
        code = jnp.where(at0, code0, jnp.where(at1, code1, 0.0))
        grad = jnp.where(at0, grad0, jnp.where(at1, grad1, 0.0))
        left_ref[base : base + count, :] = code.astype(BF16)
        left_ref[base + count : base + 2 * count, :] = grad.astype(BF16)
        along = along + (high + low)
    start = pl.multiple_of(lax.axis_index("dp") * cols, LANES)
    copies = []
    which, first = 0, 0
    for at in range(lat_rows // LANES):
        if at * LANES == first + units[which].shape[0]:
            first, which = at * LANES, which + 1
        rows = pl.ds(at * LANES, LANES)
        outer = lax.dot_general(
            left_ref[:, rows],
            right_ref[...],
            (((0,), (0,)), ((), ())),
            preferred_element_type=F32,
        )
        column = jnp.broadcast_to(along[:, at * LANES : (at + 1) * LANES], (LANES, LANES)).T
        part = pl.ds(at * LANES - first, LANES)
        unit = units[which][part, pl.ds(start, cols)].astype(F32)
        inverse = 1.0 / norms[which][part, :]
        held_ref[rows, :] = (outer - unit * column[:, :1]) * inverse
        copies.append(pltpu.make_async_copy(held_ref.at[rows], out_ref.at[rows], sems.at[at]))
        copies[-1].start()
    for copy in copies:
        copy.wait()


def gradient(count, units, norms, packets):
    lat_rows = sum(unit.shape[0] for unit in units)
    cols = packets[0].shape[1]
    depth = 2 * count * len(packets)
    return pl.pallas_call(
        functools.partial(gradient_kernel, count, len(units)),
        name="gradient",
        out_shape=shape((lat_rows, cols), F32),
        in_specs=[VMEM] * (2 * len(units) + len(packets)),
        out_specs=HBM,
        scratch_shapes=[
            pltpu.VMEM((depth, lat_rows), BF16),
            pltpu.VMEM((depth, cols), BF16),
            pltpu.VMEM((lat_rows, cols), F32),
            pltpu.SemaphoreType.DMA((lat_rows // LANES,)),
        ],
        compiler_params=params(24),
        cost_estimate=pl.CostEstimate(
            flops=2 * depth * lat_rows * cols, bytes_accessed=8 * lat_rows * cols, transcendentals=0
        ),
    )(*units, *norms, *packets)


def local(inputs, blocks, weights, enc_bias, dec_bias):
    rows_dev = inputs.shape[0]
    top = blocks.shape[1]
    chips = lax.axis_size("latent") // 2
    groups = lax.axis_size("dp")
    count = 2 * chips * rows_dev
    dec, enc = dec_bias[None, :], enc_bias[None, :]

    mate, mate_names = swap(inputs, "latent", 1), swap(blocks, "latent", 1)
    *head, own, names = normalize("normalize_a", weights, 0, HEAD, (inputs, blocks), True, 50)
    both = pack(own, mate, names, mate_names)
    pieces = [both] + [swap(both, "latent", 2 * k) for k in range(1, chips)]
    tail = normalize(
        "normalize_b", weights, HEAD, weights.shape[0] - HEAD, (both, names), False, 44
    )
    units, turneds, norms = zip(head, tail)
    contrib, cent, rows, codes, base, act, hit = forward(
        rows_dev, top, dec, enc, units, turneds, pieces
    )
    sums, sent = combine(contrib, swap(contrib, "latent", 1))
    block_scores, gate, second, compact = side(rows_dev, act, hit, codes, base, enc)
    known = (codes, base, gate, second, compact)
    if chips <= DIRECT:
        parts = [swap(sent, "latent", 2 * j) for j in range(1, chips)]
        recon, *packets = backward(
            groups, rows_dev, turneds, cent, (*known, dec, rows, sums, *parts)
        )
    else:
        full = dec_bias + sums[:rows_dev]
        for j in range(1, chips):
            full = full + swap(sums[j * rows_dev : (j + 1) * rows_dev], "latent", 2 * j)
        recon = full.astype(BF16)
        errors = (full - rows[:rows_dev].astype(F32)).astype(BF16)
        errors = [errors] + [swap(errors, "latent", 2 * j) for j in range(1, chips)]
        errors = jnp.concatenate(errors, axis=0)
        errors = jnp.concatenate([errors, swap(errors, "latent", 1)], axis=0)
        packets = backward(groups, 0, turneds, cent, (*known, errors))
    packets = [swap(p, "dp", k) if k else p for k, p in enumerate(packets)]
    grad_weights = gradient(count, units, norms, packets)
    return (recon, grad_weights, block_scores)


def solution(mesh):
    in_specs = (
        P(("dp", "latent"), None),
        P(("dp", "latent"), None),
        P("latent", None),
        P("latent"),
        P(),
    )
    out_specs = (P(("dp", "latent"), None), P("latent", "dp"), P("latent", "dp"))
    return jax.shard_map(local, mesh=mesh, in_specs=in_specs, out_specs=out_specs, check_vma=False)
```

```python
import functools

import jax
import jax.numpy as jnp
from jax import lax
from jax.experimental import pallas as pl
from jax.experimental.pallas import tpu as pltpu
from jax.sharding import PartitionSpec as P

BLK = 64
CAP = 2
RADIX = 32
LANES = 128
DIRECT = 4
TERMS = 8
VMEM = pl.BlockSpec(memory_space=pltpu.VMEM)
HBM = pl.BlockSpec(memory_space=pltpu.MemorySpace.HBM)
ANY = pl.BlockSpec(memory_space=pl.ANY)
F32, BF16 = jnp.float32, jnp.bfloat16
COST = pl.CostEstimate(flops=2**34, bytes_accessed=16 * 2**20, transcendentals=2**24)


def swap(x, axis, mask):
    size = lax.axis_size(axis)
    return lax.ppermute(x, axis, [(i, i ^ mask) for i in range(size)])


def params(mib):
    return pltpu.CompilerParams(vmem_limit_bytes=mib * 2**20)


def shape(dims, dtype):
    return jax.ShapeDtypeStruct(dims, dtype)


def stage_kernel(rows_ref, names_ref, out_ref):
    rows_dev, width = rows_ref.shape
    lane = lax.broadcasted_iota(jnp.int32, (rows_dev, LANES), 1)
    out_ref[:, :width] = rows_ref[...]
    out_ref[:, width:] = coded(names_ref[...], lane).astype(F32).astype(BF16)


def stage(rows, names):
    rows_dev, width = rows.shape
    return pl.pallas_call(
        stage_kernel,
        name="stage",
        out_shape=shape((rows_dev, width + LANES), BF16),
        in_specs=[VMEM] * 2,
        out_specs=VMEM,
        compiler_params=params(4),
        cost_estimate=COST,
    )(rows, names)


def pack_kernel(own_ref, mate_ref, mate_names_ref, out_ref):
    rows_dev, width = mate_ref.shape
    lane = lax.broadcasted_iota(jnp.int32, (rows_dev, LANES), 1)
    out_ref[:rows_dev, :] = own_ref[...]
    out_ref[rows_dev:, :width] = mate_ref[...]
    out_ref[rows_dev:, width:] = coded(mate_names_ref[...], lane).astype(F32).astype(BF16)


def coded(names, lane):
    top = names.shape[1]
    value = jnp.zeros(lane.shape, jnp.int32)
    for k in range(top):
        name = names[:, k : k + 1]
        value = jnp.where(lane == k, name // RADIX, value)
        value = jnp.where(lane == top + k, name % RADIX, value)
    return value


def pack(own, mate, mate_names):
    rows_dev, width = mate.shape
    return pl.pallas_call(
        pack_kernel,
        name="pack",
        out_shape=shape((2 * rows_dev, width + LANES), BF16),
        in_specs=[VMEM] * 3,
        out_specs=VMEM,
        compiler_params=params(4),
        cost_estimate=COST,
    )(own, mate, mate_names)


def normalize_kernel(after_ref, weights_ref, unit_ref, turned_ref, norms_ref):
    del after_ref
    lat_rows, width = weights_ref.shape
    for top in range(0, lat_rows, LANES):
        rows = pl.ds(top, LANES)
        squares = jnp.zeros((LANES, LANES), F32)
        for left in range(0, width, LANES):
            tile = weights_ref[rows, left : left + LANES].astype(F32)
            squares = squares + tile * tile
        norms = jnp.sqrt(jnp.sum(squares, axis=1, keepdims=True) + 1e-06)
        norms_ref[rows, :] = norms
        scale = jnp.broadcast_to(1.0 / norms, (LANES, LANES))
        for left in range(0, width, LANES):
            tile = weights_ref[rows, left : left + LANES].astype(F32)
            unit = (tile * scale).astype(BF16)
            unit_ref[rows, left : left + LANES] = unit
            turned_ref[left : left + LANES, rows] = unit.T


def normalize(after, weights):
    lat_rows, width = weights.shape
    return pl.pallas_call(
        normalize_kernel,
        name="normalize",
        out_shape=(
            shape((lat_rows, width), BF16),
            shape((width, lat_rows), BF16),
            shape((lat_rows, 1), F32),
        ),
        in_specs=[ANY, VMEM],
        out_specs=(VMEM,) * 3,
        compiler_params=params(20),
        cost_estimate=pl.CostEstimate(
            flops=4 * lat_rows * width, bytes_accessed=6 * lat_rows * width, transcendentals=0
        ),
    )(after, weights)


def forward_kernel(rows_dev, top, splits, dec_ref, enc_ref, *refs):
    units, turneds, refs = refs[:splits], refs[splits : 2 * splits], refs[2 * splits :]
    chips = len(refs) - 8
    pieces = refs[:chips]
    contrib_ref, cent_ref, input_ref, codes_ref, base_ref, act_ref, hit_ref, rows_ref = refs[chips:]
    half = chips * rows_dev
    width, lat_rows = units[0].shape[1], base_ref.shape[1]
    for k, piece in enumerate(pieces):
        value = piece[...].astype(F32)
        rows_ref[k * rows_dev : (k + 1) * rows_dev, :] = value[:rows_dev]
        rows_ref[half + k * rows_dev : half + (k + 1) * rows_dev, :] = value[rows_dev:]
    input_ref[...] = rows_ref[:, :width].astype(BF16)
    centered = (rows_ref[:, :width] - dec_ref[...]).astype(BF16)
    cent_ref[...] = centered
    base = times(centered, turneds)
    base_ref[...] = base
    preact = base + enc_ref[...]
    act = jnp.maximum(preact, 0.0) + jnp.log1p(jnp.exp(-jnp.abs(preact)))
    act_ref[...] = act
    first = lax.axis_index("latent") * (lat_rows // BLK)
    lat = lax.broadcasted_iota(jnp.int32, (2 * half, lat_rows), 1)
    block_of = (first + lat // BLK).astype(F32)
    names = rows_ref[:, width:]
    hit = jnp.zeros((2 * half, lat_rows), F32)
    for k in range(top):
        name = names[:, k : k + 1] * RADIX + names[:, top + k : top + k + 1]
        hit = jnp.where(name == block_of, 1.0, hit)
    hit_ref[...] = hit
    codes = (act * hit).astype(BF16)
    codes_ref[...] = codes
    at, contrib = 0, None
    for unit in units:
        part = codes[:, at : at + unit.shape[0]]
        term = jnp.dot(part, unit[...], preferred_element_type=F32)
        contrib = term if contrib is None else contrib + term
        at += unit.shape[0]
    contrib_ref[...] = contrib


def times(x, parts):
    return jnp.concatenate(
        [jnp.dot(x, part[...], preferred_element_type=F32) for part in parts], axis=1
    )


def forward(rows_dev, top, dec, enc, units, turneds, pieces):
    lat_rows, width = enc.shape[1], units[0].shape[1]
    count = 2 * len(pieces) * rows_dev
    return pl.pallas_call(
        functools.partial(forward_kernel, rows_dev, top, len(units)),
        name="forward",
        out_shape=(
            shape((count, width), F32),
            shape((count, width), BF16),
            shape((count, width), BF16),
            shape((count, lat_rows), BF16),
            shape((count, lat_rows), F32),
            shape((count, lat_rows), F32),
            shape((count, lat_rows), F32),
        ),
        in_specs=[VMEM] * (2 + 2 * len(units) + len(pieces)),
        out_specs=(VMEM,) * 7,
        scratch_shapes=[pltpu.VMEM((count, width + LANES), F32)],
        compiler_params=params(20),
        cost_estimate=pl.CostEstimate(
            flops=4 * count * lat_rows * width,
            bytes_accessed=4 * lat_rows * width,
            transcendentals=2 * count * lat_rows,
        ),
    )(dec, enc, *units, *turneds, *pieces)


def side_kernel(rows_dev, act_ref, hit_ref, codes_ref, base_ref, enc_ref, *outs):
    scores_ref, gate_ref, second_ref, compact_ref = outs
    count, lat_rows = act_ref.shape
    block_count = lat_rows // BLK
    half = count // 2
    me = lax.axis_index("latent")
    latent = lax.broadcasted_iota(jnp.int32, (block_count, lat_rows), 1)
    block = lax.broadcasted_iota(jnp.int32, (block_count, lat_rows), 0)
    inside = jnp.where(latent // BLK == block, 1.0 / BLK, 0.0).astype(F32)
    means = lax.dot_general(
        inside,
        act_ref[...],
        (((1,), (1,)), ((), ())),
        preferred_element_type=F32,
        precision=lax.Precision.HIGHEST,
    )
    at = lax.broadcasted_iota(jnp.int32, (count, count), 0)
    place = lax.broadcasted_iota(jnp.int32, (count, count), 1)
    owner = (place // rows_dev) ^ me
    relative = (owner % 2) * half + (owner // 2) * rows_dev + place % rows_dev
    order = jnp.where(relative == at, 1.0, 0.0).astype(F32)
    scores_ref[...] = jnp.dot(
        means, order, preferred_element_type=F32, precision=lax.Precision.HIGHEST
    )
    hit = hit_ref[...]
    preact = base_ref[...] + enc_ref[...]
    gate_ref[...] = hit * jax.nn.sigmoid(preact)
    earlier = jnp.where(place < at, 1.0, 0.0).astype(BF16)
    before = jnp.dot(earlier, hit.astype(BF16), preferred_element_type=F32)
    second = jnp.where(before == 1.0, hit, 0.0)
    first = jnp.where(before == 0.0, hit, 0.0)
    second_ref[...] = second
    codes = codes_ref[...].astype(F32)
    number = (lax.broadcasted_iota(jnp.int32, (count, lat_rows), 0) + 1).astype(F32)
    rows = []
    for slot in (first, second):
        rows.append(jnp.sum(slot * codes, axis=0, keepdims=True))
    for slot in (first, second):
        rows.append(jnp.sum(slot * number, axis=0, keepdims=True))
    for at, row in enumerate(rows):
        compact_ref[at : at + 1, :] = row


def side(rows_dev, act, hit, codes, base, enc):
    count, lat_rows = act.shape
    return pl.pallas_call(
        functools.partial(side_kernel, rows_dev),
        name="side",
        out_shape=(
            shape((lat_rows // BLK, count), F32),
            shape((count, lat_rows), F32),
            shape((count, lat_rows), F32),
            shape((2 * CAP, lat_rows), F32),
        ),
        in_specs=[VMEM] * 5,
        out_specs=(VMEM,) * 4,
        compiler_params=params(20),
        cost_estimate=pl.CostEstimate(
            flops=8 * count * lat_rows * 64, bytes_accessed=32 * count * lat_rows, transcendentals=0
        ),
    )(act, hit, codes, base, enc)


def combine_kernel(mine_ref, mate_ref, sums_ref, sent_ref):
    half = mine_ref.shape[0] // 2
    for at, other in ((0, half), (half, 0)):
        sums = mine_ref[at : at + half, :] + mate_ref[other : other + half, :]
        sums_ref[at : at + half, :] = sums
        sent_ref[at : at + half, :] = sums.astype(BF16)


def combine(mine, mate):
    return pl.pallas_call(
        combine_kernel,
        name="combine",
        out_shape=(shape(mine.shape, F32), shape(mine.shape, BF16)),
        in_specs=[VMEM] * 2,
        out_specs=(VMEM, VMEM),
        compiler_params=params(12),
    )(mine, mate)


def errors_kernel(rows_dev, dec_ref, input_ref, sums_ref, parts, recon_ref, errors_ref):
    chips = len(parts) + 1
    total = sums_ref[...]
    for j, part in enumerate(parts, 1):
        value = part[...].astype(F32)
        turned = []
        for k in range(2 * chips):
            at = (k ^ j) * rows_dev
            turned.append(value[at : at + rows_dev])
        total = total + jnp.concatenate(turned, axis=0)
    full = total + dec_ref[...]
    recon_ref[...] = full[:rows_dev].astype(BF16)
    errors_ref[...] = (full - input_ref[...].astype(F32)).astype(BF16)


def backward_kernel(groups, rows_dev, splits, *refs):
    turneds, refs = refs[:splits], refs[splits:]
    cent_ref, codes_ref, base_ref, gate_ref = refs[:4]
    refs = refs[4:]
    second_ref, compact_ref = refs[:2]
    if rows_dev:
        chips = cent_ref.shape[0] // (2 * rows_dev)
        dec_ref, input_ref, sums_ref = refs[2:5]
        parts, outs = refs[5 : 4 + chips], refs[4 + chips :]
        recon_ref, packets, errors_ref = outs[0], outs[1:-1], outs[-1]
        errors_kernel(rows_dev, dec_ref, input_ref, sums_ref, parts, recon_ref, errors_ref)
    else:
        errors_ref, packets = refs[2], refs[3:]
    count, width = cent_ref.shape
    lat_rows = codes_ref.shape[1]
    cols = width // groups
    grad = times(errors_ref[...], turneds)
    pre_grad = (grad * gate_ref[...]).astype(BF16).astype(F32)
    codes = codes_ref[...].astype(F32)
    along = jnp.sum(codes * grad + pre_grad * base_ref[...], axis=0, keepdims=True)
    high = along.astype(BF16).astype(F32)
    both = jnp.sum(pre_grad, axis=0, keepdims=True)
    later = jnp.sum(pre_grad * second_ref[...], axis=0, keepdims=True)
    table = compact_ref[...]
    terms = jnp.concatenate([table, both - later, later, high, along - high], axis=0).astype(BF16)
    group = lax.axis_index("dp")
    for k, packet in enumerate(packets):
        at = pl.ds(pl.multiple_of((group ^ k) * cols, LANES), cols)
        packet[:count, :] = errors_ref[:, at]
        packet[count : 2 * count, :] = cent_ref[:, at]
        for part in range(lat_rows // cols):
            rows = pl.ds(2 * count + part * TERMS, TERMS)
            packet[rows, :] = terms[:, part * cols : (part + 1) * cols]


def backward(groups, rows_dev, turneds, cent, rest):
    count, width = cent.shape
    lat_rows = rest[0].shape[1]
    cols = width // groups
    packet = shape((2 * count + TERMS * lat_rows // cols, cols), BF16)
    outs = (packet,) * groups
    scratch = []
    if rows_dev:
        outs = (shape((rows_dev, width), BF16),) + outs
        scratch = [pltpu.VMEM((count, width), BF16)]
    return pl.pallas_call(
        functools.partial(backward_kernel, groups, rows_dev, len(turneds)),
        name="backward",
        out_shape=outs,
        in_specs=[VMEM] * (len(turneds) + 1 + len(rest)),
        out_specs=(VMEM,) * len(outs),
        scratch_shapes=scratch,
        compiler_params=params(20),
        cost_estimate=pl.CostEstimate(
            flops=2 * count * lat_rows * width, bytes_accessed=2 * lat_rows * width, transcendentals=0
        ),
    )(*turneds, cent, *rest)


def gradient_kernel(count, splits, *refs):
    units, norms, refs = refs[:splits], refs[splits : 2 * splits], refs[2 * splits :]
    out_ref, left_ref, right_ref, held_ref, sems = refs[-5:]
    packets = refs[:-5]
    lat_rows, cols = out_ref.shape
    along = jnp.zeros((1, lat_rows), F32)
    number = (lax.broadcasted_iota(jnp.int32, (count, lat_rows), 0) + 1).astype(F32)
    for g, packet in enumerate(packets):
        base = g * 2 * count
        right_ref[base : base + 2 * count, :] = packet[: 2 * count, :]
        parts = [
            packet[2 * count + p * TERMS : 2 * count + (p + 1) * TERMS, :].astype(F32)
            for p in range(lat_rows // cols)
        ]
        terms = jnp.concatenate(parts, axis=1)
        code0, code1, row0, row1, grad0, grad1, high, low = [
            terms[t : t + 1] for t in range(TERMS)
        ]
        at0, at1 = number == row0, number == row1
        code = jnp.where(at0, code0, jnp.where(at1, code1, 0.0))
        grad = jnp.where(at0, grad0, jnp.where(at1, grad1, 0.0))
        left_ref[base : base + count, :] = code.astype(BF16)
        left_ref[base + count : base + 2 * count, :] = grad.astype(BF16)
        along = along + (high + low)
    start = pl.multiple_of(lax.axis_index("dp") * cols, LANES)
    copies = []
    which, first = 0, 0
    for at in range(lat_rows // LANES):
        if at * LANES == first + units[which].shape[0]:
            first, which = at * LANES, which + 1
        rows = pl.ds(at * LANES, LANES)
        outer = lax.dot_general(
            left_ref[:, rows],
            right_ref[...],
            (((0,), (0,)), ((), ())),
            preferred_element_type=F32,
        )
        column = jnp.broadcast_to(along[:, at * LANES : (at + 1) * LANES], (LANES, LANES)).T
        part = pl.ds(at * LANES - first, LANES)
        unit = units[which][part, pl.ds(start, cols)].astype(F32)
        inverse = 1.0 / norms[which][part, :]
        held_ref[rows, :] = (outer - unit * column[:, :1]) * inverse
        copies.append(pltpu.make_async_copy(held_ref.at[rows], out_ref.at[rows], sems.at[at]))
        copies[-1].start()
    for copy in copies:
        copy.wait()


def gradient(count, units, norms, packets):
    lat_rows = sum(unit.shape[0] for unit in units)
    cols = packets[0].shape[1]
    depth = 2 * count * len(packets)
    return pl.pallas_call(
        functools.partial(gradient_kernel, count, len(units)),
        name="gradient",
        out_shape=shape((lat_rows, cols), F32),
        in_specs=[VMEM] * (2 * len(units) + len(packets)),
        out_specs=HBM,
        scratch_shapes=[
            pltpu.VMEM((depth, lat_rows), BF16),
            pltpu.VMEM((depth, cols), BF16),
            pltpu.VMEM((lat_rows, cols), F32),
            pltpu.SemaphoreType.DMA((lat_rows // LANES,)),
        ],
        compiler_params=params(24),
        cost_estimate=pl.CostEstimate(
            flops=2 * depth * lat_rows * cols, bytes_accessed=8 * lat_rows * cols, transcendentals=0
        ),
    )(*units, *norms, *packets)


def local(inputs, blocks, weights, enc_bias, dec_bias):
    rows_dev = inputs.shape[0]
    top = blocks.shape[1]
    chips = lax.axis_size("latent") // 2
    groups = lax.axis_size("dp")
    count = 2 * chips * rows_dev
    dec, enc = dec_bias[None, :], enc_bias[None, :]

    mate, mate_names = swap(inputs, "latent", 1), swap(blocks, "latent", 1)
    both = pack(stage(inputs, blocks), mate, mate_names)
    pieces = [both] + [swap(both, "latent", 2 * k) for k in range(1, chips)]
    units, turneds, norms = ([x] for x in normalize(both, weights))
    contrib, cent, rows, codes, base, act, hit = forward(
        rows_dev, top, dec, enc, units, turneds, pieces
    )
    sums, sent = combine(contrib, swap(contrib, "latent", 1))
    block_scores, gate, second, compact = side(rows_dev, act, hit, codes, base, enc)
    known = (codes, base, gate, second, compact)
    if chips <= DIRECT:
        parts = [swap(sent, "latent", 2 * j) for j in range(1, chips)]
        recon, *packets = backward(
            groups, rows_dev, turneds, cent, (*known, dec, rows, sums, *parts)
        )
    else:
        full = dec_bias + sums[:rows_dev]
        for j in range(1, chips):
            full = full + swap(sums[j * rows_dev : (j + 1) * rows_dev], "latent", 2 * j)
        recon = full.astype(BF16)
        errors = (full - rows[:rows_dev].astype(F32)).astype(BF16)
        errors = [errors] + [swap(errors, "latent", 2 * j) for j in range(1, chips)]
        errors = jnp.concatenate(errors, axis=0)
        errors = jnp.concatenate([errors, swap(errors, "latent", 1)], axis=0)
        packets = backward(groups, 0, turneds, cent, (*known, errors))
    packets = [swap(p, "dp", k) if k else p for k, p in enumerate(packets)]
    grad_weights = gradient(count, units, norms, packets)
    return (recon, grad_weights, block_scores)


def solution(mesh):
    in_specs = (
        P(("dp", "latent"), None),
        P(("dp", "latent"), None),
        P("latent", None),
        P("latent"),
        P(),
    )
    out_specs = (P(("dp", "latent"), None), P("latent", "dp"), P("latent", "dp"))
    return jax.shard_map(local, mesh=mesh, in_specs=in_specs, out_specs=out_specs, check_vma=False)
```

```python
import functools

import jax
import jax.numpy as jnp
from jax import lax
from jax.experimental import pallas as pl
from jax.experimental.pallas import tpu as pltpu
from jax.sharding import PartitionSpec as P

BLK = 64
CAP = 2
RADIX = 32
LANES = 128
DIRECT = 4
TERMS = 8
ORDER = (0, 1, 2, 3)
ORDER_DP = (0, 1, 3, 2)
VMEM = pl.BlockSpec(memory_space=pltpu.VMEM)
HBM = pl.BlockSpec(memory_space=pltpu.MemorySpace.HBM)
ANY = pl.BlockSpec(memory_space=pl.ANY)
F32, BF16 = jnp.float32, jnp.bfloat16
COST = pl.CostEstimate(flops=2**34, bytes_accessed=16 * 2**20, transcendentals=2**24)


def swap(x, axis, mask):
    size = lax.axis_size(axis)
    return lax.ppermute(x, axis, [(i, i ^ mask) for i in range(size)])


def swaps(xs, axis, step):
    return [swap(x, axis, step * k) if k else x for k, x in enumerate(xs)]


def taken(order, xs):
    return tuple(xs[k] for k in ranked(order, len(xs)))


def ranked(order, count):
    return order if len(order) == count else tuple(range(count))


def restored(order, refs):
    order = ranked(order, len(refs))
    return [refs[order.index(k)] for k in range(len(refs))]


def params(mib):
    return pltpu.CompilerParams(vmem_limit_bytes=mib * 2**20)


def shape(dims, dtype):
    return jax.ShapeDtypeStruct(dims, dtype)


def stage_kernel(rows_ref, names_ref, out_ref):
    rows_dev, width = rows_ref.shape
    lane = lax.broadcasted_iota(jnp.int32, (rows_dev, LANES), 1)
    out_ref[:, :width] = rows_ref[...]
    out_ref[:, width:] = coded(names_ref[...], lane).astype(F32).astype(BF16)


def stage(rows, names):
    rows_dev, width = rows.shape
    return pl.pallas_call(
        stage_kernel,
        name="stage",
        out_shape=shape((rows_dev, width + LANES), BF16),
        in_specs=[VMEM] * 2,
        out_specs=VMEM,
        compiler_params=params(4),
        cost_estimate=COST,
    )(rows, names)


def pack_kernel(own_ref, mate_ref, mate_names_ref, out_ref):
    rows_dev, width = mate_ref.shape
    lane = lax.broadcasted_iota(jnp.int32, (rows_dev, LANES), 1)
    out_ref[:rows_dev, :] = own_ref[...]
    out_ref[rows_dev:, :width] = mate_ref[...]
    out_ref[rows_dev:, width:] = coded(mate_names_ref[...], lane).astype(F32).astype(BF16)


def coded(names, lane):
    top = names.shape[1]
    value = jnp.zeros(lane.shape, jnp.int32)
    for k in range(top):
        name = names[:, k : k + 1]
        value = jnp.where(lane == k, name // RADIX, value)
        value = jnp.where(lane == top + k, name % RADIX, value)
    return value


def pack(own, mate, mate_names):
    rows_dev, width = mate.shape
    return pl.pallas_call(
        pack_kernel,
        name="pack",
        out_shape=shape((2 * rows_dev, width + LANES), BF16),
        in_specs=[VMEM] * 3,
        out_specs=VMEM,
        compiler_params=params(4),
        cost_estimate=COST,
    )(own, mate, mate_names)


def normalize_kernel(after_ref, weights_ref, unit_ref, turned_ref, norms_ref):
    del after_ref
    lat_rows, width = weights_ref.shape
    for top in range(0, lat_rows, LANES):
        rows = pl.ds(top, LANES)
        squares = jnp.zeros((LANES, LANES), F32)
        for left in range(0, width, LANES):
            tile = weights_ref[rows, left : left + LANES].astype(F32)
            squares = squares + tile * tile
        norms = jnp.sqrt(jnp.sum(squares, axis=1, keepdims=True) + 1e-06)
        norms_ref[rows, :] = norms
        scale = jnp.broadcast_to(1.0 / norms, (LANES, LANES))
        for left in range(0, width, LANES):
            tile = weights_ref[rows, left : left + LANES].astype(F32)
            unit = (tile * scale).astype(BF16)
            unit_ref[rows, left : left + LANES] = unit
            turned_ref[left : left + LANES, rows] = unit.T


def normalize(after, weights):
    lat_rows, width = weights.shape
    return pl.pallas_call(
        normalize_kernel,
        name="normalize",
        out_shape=(
            shape((lat_rows, width), BF16),
            shape((width, lat_rows), BF16),
            shape((lat_rows, 1), F32),
        ),
        in_specs=[ANY, VMEM],
        out_specs=(VMEM,) * 3,
        compiler_params=params(20),
        cost_estimate=pl.CostEstimate(
            flops=4 * lat_rows * width, bytes_accessed=6 * lat_rows * width, transcendentals=0
        ),
    )(after, weights)


def forward_kernel(rows_dev, top, splits, dec_ref, enc_ref, *refs):
    units, turneds, refs = refs[:splits], refs[splits : 2 * splits], refs[2 * splits :]
    chips = len(refs) - 8
    pieces = restored(ORDER, refs[:chips])
    contrib_ref, cent_ref, input_ref, codes_ref, base_ref, act_ref, hit_ref, rows_ref = refs[chips:]
    count = 2 * chips * rows_dev
    width, lat_rows = units[0].shape[1], base_ref.shape[1]
    for k, piece in enumerate(pieces):
        rows_ref[2 * k * rows_dev : 2 * (k + 1) * rows_dev, :] = piece[...].astype(F32)
    input_ref[...] = rows_ref[:, :width].astype(BF16)
    centered = (rows_ref[:, :width] - dec_ref[...]).astype(BF16)
    cent_ref[...] = centered
    base = times(centered, turneds)
    base_ref[...] = base
    preact = base + enc_ref[...]
    act = jnp.maximum(preact, 0.0) + jnp.log1p(jnp.exp(-jnp.abs(preact)))
    act_ref[...] = act
    first = lax.axis_index("latent") * (lat_rows // BLK)
    lat = lax.broadcasted_iota(jnp.int32, (count, lat_rows), 1)
    block_of = (first + lat // BLK).astype(F32)
    names = rows_ref[:, width:]
    hit = jnp.zeros((count, lat_rows), F32)
    for k in range(top):
        name = names[:, k : k + 1] * RADIX + names[:, top + k : top + k + 1]
        hit = jnp.where(name == block_of, 1.0, hit)
    hit_ref[...] = hit
    codes = (act * hit).astype(BF16)
    codes_ref[...] = codes
    at, contrib = 0, None
    for unit in units:
        part = codes[:, at : at + unit.shape[0]]
        term = jnp.dot(part, unit[...], preferred_element_type=F32)
        contrib = term if contrib is None else contrib + term
        at += unit.shape[0]
    contrib_ref[...] = contrib


def times(x, parts):
    return jnp.concatenate(
        [jnp.dot(x, part[...], preferred_element_type=F32) for part in parts], axis=1
    )


def forward(rows_dev, top, dec, enc, units, turneds, pieces):
    lat_rows, width = enc.shape[1], units[0].shape[1]
    count = 2 * len(pieces) * rows_dev
    return pl.pallas_call(
        functools.partial(forward_kernel, rows_dev, top, len(units)),
        name="forward",
        out_shape=(
            shape((count, width), F32),
            shape((count, width), BF16),
            shape((count, width), BF16),
            shape((count, lat_rows), BF16),
            shape((count, lat_rows), F32),
            shape((count, lat_rows), F32),
            shape((count, lat_rows), F32),
        ),
        in_specs=[VMEM] * (2 + 2 * len(units) + len(pieces)),
        out_specs=(VMEM,) * 7,
        scratch_shapes=[pltpu.VMEM((count, width + LANES), F32)],
        compiler_params=params(20),
        cost_estimate=pl.CostEstimate(
            flops=4 * count * lat_rows * width,
            bytes_accessed=4 * lat_rows * width,
            transcendentals=2 * count * lat_rows,
        ),
    )(dec, enc, *units, *turneds, *taken(ORDER, pieces))


def side_kernel(rows_dev, act_ref, hit_ref, codes_ref, base_ref, enc_ref, *outs):
    scores_ref, gate_ref, second_ref, compact_ref = outs
    count, lat_rows = act_ref.shape
    block_count = lat_rows // BLK
    me = lax.axis_index("latent")
    latent = lax.broadcasted_iota(jnp.int32, (block_count, lat_rows), 1)
    block = lax.broadcasted_iota(jnp.int32, (block_count, lat_rows), 0)
    inside = jnp.where(latent // BLK == block, 1.0 / BLK, 0.0).astype(F32)
    means = lax.dot_general(
        inside,
        act_ref[...],
        (((1,), (1,)), ((), ())),
        preferred_element_type=F32,
        precision=lax.Precision.HIGHEST,
    )
    at = lax.broadcasted_iota(jnp.int32, (count, count), 0)
    place = lax.broadcasted_iota(jnp.int32, (count, count), 1)
    relative = ((place // rows_dev) ^ me) * rows_dev + place % rows_dev
    order = jnp.where(relative == at, 1.0, 0.0).astype(F32)
    scores_ref[...] = jnp.dot(
        means, order, preferred_element_type=F32, precision=lax.Precision.HIGHEST
    )
    hit = hit_ref[...]
    preact = base_ref[...] + enc_ref[...]
    gate_ref[...] = hit * jax.nn.sigmoid(preact)
    earlier = jnp.where(place < at, 1.0, 0.0).astype(BF16)
    before = jnp.dot(earlier, hit.astype(BF16), preferred_element_type=F32)
    second = jnp.where(before == 1.0, hit, 0.0)
    first = jnp.where(before == 0.0, hit, 0.0)
    second_ref[...] = second
    codes = codes_ref[...].astype(F32)
    number = (lax.broadcasted_iota(jnp.int32, (count, lat_rows), 0) + 1).astype(F32)
    rows = []
    for slot in (first, second):
        rows.append(jnp.sum(slot * codes, axis=0, keepdims=True))
    for slot in (first, second):
        rows.append(jnp.sum(slot * number, axis=0, keepdims=True))
    for at, row in enumerate(rows):
        compact_ref[at : at + 1, :] = row


def side(rows_dev, act, hit, codes, base, enc):
    count, lat_rows = act.shape
    return pl.pallas_call(
        functools.partial(side_kernel, rows_dev),
        name="side",
        out_shape=(
            shape((lat_rows // BLK, count), F32),
            shape((count, lat_rows), F32),
            shape((count, lat_rows), F32),
            shape((2 * CAP, lat_rows), F32),
        ),
        in_specs=[VMEM] * 5,
        out_specs=(VMEM,) * 4,
        compiler_params=params(20),
        cost_estimate=pl.CostEstimate(
            flops=8 * count * lat_rows * 64, bytes_accessed=32 * count * lat_rows, transcendentals=0
        ),
    )(act, hit, codes, base, enc)


def exchanged(value, step, mask):
    blocks = range(value.shape[0] // step)
    return jnp.concatenate(
        [value[(k ^ mask) * step : ((k ^ mask) + 1) * step] for k in blocks], axis=0
    )


def combine_kernel(rows_dev, mine_ref, mate_ref, sums_ref, sent_ref):
    sums = mine_ref[...] + exchanged(mate_ref[...], rows_dev, 1)
    sums_ref[...] = sums
    sent_ref[...] = sums.astype(BF16)


def combine(rows_dev, mine, mate):
    return pl.pallas_call(
        functools.partial(combine_kernel, rows_dev),
        name="combine",
        out_shape=(shape(mine.shape, F32), shape(mine.shape, BF16)),
        in_specs=[VMEM] * 2,
        out_specs=(VMEM, VMEM),
        compiler_params=params(12),
    )(mine, mate)


def errors_kernel(rows_dev, dec_ref, input_ref, parts, recon_ref, errors_ref):
    total = parts[0][...]
    for j in range(1, len(parts)):
        total = total + exchanged(parts[j][...].astype(F32), 2 * rows_dev, j)
    full = total + dec_ref[...]
    recon_ref[...] = full[:rows_dev]
    errors_ref[...] = (full - input_ref[...].astype(F32)).astype(BF16)


def backward_kernel(groups, rows_dev, splits, *refs):
    turneds, refs = refs[:splits], refs[splits:]
    cent_ref, codes_ref, base_ref, gate_ref = refs[:4]
    refs = refs[4:]
    second_ref, compact_ref = refs[:2]
    if rows_dev:
        chips = cent_ref.shape[0] // (2 * rows_dev)
        dec_ref, input_ref = refs[2:4]
        parts, outs = restored(ORDER, refs[4 : 4 + chips]), refs[4 + chips :]
        recon_ref, packets, errors_ref = outs[0], outs[1:-1], outs[-1]
        errors_kernel(rows_dev, dec_ref, input_ref, parts, recon_ref, errors_ref)
    else:
        errors_ref, packets = refs[2], refs[3:]
    count, width = cent_ref.shape
    lat_rows = codes_ref.shape[1]
    cols = width // groups
    grad = times(errors_ref[...], turneds)
    pre_grad = (grad * gate_ref[...]).astype(BF16).astype(F32)
    codes = codes_ref[...].astype(F32)
    along = jnp.sum(codes * grad + pre_grad * base_ref[...], axis=0, keepdims=True)
    high = along.astype(BF16).astype(F32)
    both = jnp.sum(pre_grad, axis=0, keepdims=True)
    later = jnp.sum(pre_grad * second_ref[...], axis=0, keepdims=True)
    table = compact_ref[...]
    terms = jnp.concatenate([table, both - later, later, high, along - high], axis=0).astype(BF16)
    group = lax.axis_index("dp")
    for k, packet in enumerate(packets):
        at = pl.ds(pl.multiple_of((group ^ k) * cols, LANES), cols)
        packet[:count, :] = errors_ref[:, at]
        packet[count : 2 * count, :] = cent_ref[:, at]
        for part in range(lat_rows // cols):
            rows = pl.ds(2 * count + part * TERMS, TERMS)
            packet[rows, :] = terms[:, part * cols : (part + 1) * cols]


def backward(groups, rows_dev, turneds, cent, rest):
    count, width = cent.shape
    lat_rows = rest[0].shape[1]
    cols = width // groups
    packet = shape((2 * count + TERMS * lat_rows // cols, cols), BF16)
    outs = (packet,) * groups
    scratch = []
    if rows_dev:
        outs = (shape((rows_dev, width), F32),) + outs
        scratch = [pltpu.VMEM((count, width), BF16)]
    return pl.pallas_call(
        functools.partial(backward_kernel, groups, rows_dev, len(turneds)),
        name="backward",
        out_shape=outs,
        in_specs=[VMEM] * (len(turneds) + 1 + len(rest)),
        out_specs=(VMEM,) * len(outs),
        scratch_shapes=scratch,
        compiler_params=params(20),
        cost_estimate=pl.CostEstimate(
            flops=2 * count * lat_rows * width, bytes_accessed=2 * lat_rows * width, transcendentals=0
        ),
    )(*turneds, cent, *rest)


def rounded_kernel(value_ref, out_ref):
    out_ref[...] = value_ref[...].astype(BF16)


def rounded(value):
    return pl.pallas_call(
        rounded_kernel,
        name="rounded",
        out_shape=shape(value.shape, BF16),
        in_specs=[VMEM],
        out_specs=VMEM,
        compiler_params=params(4),
    )(value)


def gradient_kernel(count, splits, *refs):
    units, norms, refs = refs[:splits], refs[splits : 2 * splits], refs[2 * splits :]
    out_ref, left_ref, right_ref, held_ref, sems = refs[-5:]
    packets = restored(ORDER_DP, refs[:-5])
    lat_rows, cols = out_ref.shape
    along = jnp.zeros((1, lat_rows), F32)
    number = (lax.broadcasted_iota(jnp.int32, (count, lat_rows), 0) + 1).astype(F32)
    for g, packet in enumerate(packets):
        base = g * 2 * count
        right_ref[base : base + 2 * count, :] = packet[: 2 * count, :]
        parts = [
            packet[2 * count + p * TERMS : 2 * count + (p + 1) * TERMS, :].astype(F32)
            for p in range(lat_rows // cols)
        ]
        terms = jnp.concatenate(parts, axis=1)
        code0, code1, row0, row1, grad0, grad1, high, low = [
            terms[t : t + 1] for t in range(TERMS)
        ]
        at0, at1 = number == row0, number == row1
        code = jnp.where(at0, code0, jnp.where(at1, code1, 0.0))
        grad = jnp.where(at0, grad0, jnp.where(at1, grad1, 0.0))
        left_ref[base : base + count, :] = code.astype(BF16)
        left_ref[base + count : base + 2 * count, :] = grad.astype(BF16)
        along = along + (high + low)
    start = pl.multiple_of(lax.axis_index("dp") * cols, LANES)
    copies = []
    which, first = 0, 0
    for at in range(lat_rows // LANES):
        if at * LANES == first + units[which].shape[0]:
            first, which = at * LANES, which + 1
        rows = pl.ds(at * LANES, LANES)
        outer = lax.dot_general(
            left_ref[:, rows],
            right_ref[...],
            (((0,), (0,)), ((), ())),
            preferred_element_type=F32,
        )
        column = jnp.broadcast_to(along[:, at * LANES : (at + 1) * LANES], (LANES, LANES)).T
        part = pl.ds(at * LANES - first, LANES)
        unit = units[which][part, pl.ds(start, cols)].astype(F32)
        inverse = 1.0 / norms[which][part, :]
        held_ref[rows, :] = (outer - unit * column[:, :1]) * inverse
        copies.append(pltpu.make_async_copy(held_ref.at[rows], out_ref.at[rows], sems.at[at]))
        copies[-1].start()
    for copy in copies:
        copy.wait()


def gradient(count, units, norms, packets):
    lat_rows = sum(unit.shape[0] for unit in units)
    cols = packets[0].shape[1]
    depth = 2 * count * len(packets)
    return pl.pallas_call(
        functools.partial(gradient_kernel, count, len(units)),
        name="gradient",
        out_shape=shape((lat_rows, cols), F32),
        in_specs=[VMEM] * (2 * len(units) + len(packets)),
        out_specs=HBM,
        scratch_shapes=[
            pltpu.VMEM((depth, lat_rows), BF16),
            pltpu.VMEM((depth, cols), BF16),
            pltpu.VMEM((lat_rows, cols), F32),
            pltpu.SemaphoreType.DMA((lat_rows // LANES,)),
        ],
        compiler_params=params(24),
        cost_estimate=pl.CostEstimate(
            flops=2 * depth * lat_rows * cols, bytes_accessed=8 * lat_rows * cols, transcendentals=0
        ),
    )(*units, *norms, *taken(ORDER_DP, packets))


def local(inputs, blocks, weights, enc_bias, dec_bias):
    rows_dev = inputs.shape[0]
    top = blocks.shape[1]
    chips = lax.axis_size("latent") // 2
    groups = lax.axis_size("dp")
    count = 2 * chips * rows_dev
    dec, enc = dec_bias[None, :], enc_bias[None, :]

    mate, mate_names = swap(inputs, "latent", 1), swap(blocks, "latent", 1)
    both = pack(stage(inputs, blocks), mate, mate_names)
    pieces = swaps([both] * chips, "latent", 2)
    units, turneds, norms = ([x] for x in normalize(both, weights))
    contrib, cent, rows, codes, base, act, hit = forward(
        rows_dev, top, dec, enc, units, turneds, pieces
    )
    sums, sent = combine(rows_dev, contrib, swap(contrib, "latent", 1))
    block_scores, gate, second, compact = side(rows_dev, act, hit, codes, base, enc)
    known = (codes, base, gate, second, compact)
    if chips <= DIRECT:
        parts = [sums] + swaps([sent] * chips, "latent", 2)[1:]
        recon, *packets = backward(
            groups, rows_dev, turneds, cent, (*known, dec, rows, *taken(ORDER, parts))
        )
    else:
        full = dec_bias + sums[:rows_dev]
        for j in range(1, chips):
            at = 2 * j * rows_dev
            full = full + swap(sums[at : at + rows_dev], "latent", 2 * j)
        recon = full
        errors = (full - rows[:rows_dev].astype(F32)).astype(BF16)
        errors = jnp.concatenate([errors, swap(errors, "latent", 1)], axis=0)
        errors = jnp.concatenate(swaps([errors] * chips, "latent", 2), axis=0)
        packets = backward(groups, 0, turneds, cent, (*known, errors))
    packets = swaps(packets, "dp", 1)
    grad_weights = gradient(count, units, norms, packets)
    return (rounded(recon), grad_weights, block_scores)


def solution(mesh):
    in_specs = (
        P(("dp", "latent"), None),
        P(("dp", "latent"), None),
        P("latent", None),
        P("latent"),
        P(),
    )
    out_specs = (P(("dp", "latent"), None), P("latent", "dp"), P("latent", "dp"))
    return jax.shard_map(local, mesh=mesh, in_specs=in_specs, out_specs=out_specs, check_vma=False)
```

```python
import functools

import jax
import jax.numpy as jnp
from jax import lax
from jax.experimental import pallas as pl
from jax.experimental.pallas import tpu as pltpu
from jax.sharding import PartitionSpec as P

BLK = 64
CAP = 2
SHIFT = 5
RADIX = 1 << SHIFT
LANES = 128
DIRECT = 4
TERMS = 8
ORDER = (0, 1, 2, 3)
ORDER_DP = (0, 1, 3, 2)
VMEM = pl.BlockSpec(memory_space=pltpu.VMEM)
HBM = pl.BlockSpec(memory_space=pltpu.MemorySpace.HBM)
ANY = pl.BlockSpec(memory_space=pl.ANY)
F32, BF16 = jnp.float32, jnp.bfloat16
COST = pl.CostEstimate(flops=2**34, bytes_accessed=16 * 2**20, transcendentals=2**24)


def swap(x, axis, mask):
    size = lax.axis_size(axis)
    return lax.ppermute(x, axis, [(i, i ^ mask) for i in range(size)])


def swaps(xs, axis, step):
    return [swap(x, axis, step * k) if k else x for k, x in enumerate(xs)]


def taken(order, xs):
    return tuple(xs[k] for k in ranked(order, len(xs)))


def ranked(order, count):
    return order if len(order) == count else tuple(range(count))


def restored(order, refs):
    order = ranked(order, len(refs))
    return [refs[order.index(k)] for k in range(len(refs))]


def params(mib):
    return pltpu.CompilerParams(vmem_limit_bytes=mib * 2**20)


def shape(dims, dtype):
    return jax.ShapeDtypeStruct(dims, dtype)


def pack_kernel(own_ref, mate_ref, mate_names_ref, out_ref):
    rows_dev, width = mate_ref.shape
    lane = lax.broadcasted_iota(jnp.int32, (rows_dev, LANES), 1)
    out_ref[:rows_dev, :] = own_ref[...]
    out_ref[rows_dev:, :width] = mate_ref[...]
    out_ref[rows_dev:, width:] = coded(mate_names_ref[...], lane).astype(F32).astype(BF16)


def coded(names, lane):
    top = names.shape[1]
    value = jnp.zeros(lane.shape, jnp.int32)
    for k in range(top):
        name = names[:, k : k + 1]
        value = jnp.where(lane == k, name // RADIX, value)
        value = jnp.where(lane == top + k, name % RADIX, value)
    return value


def pack(own, mate, mate_names):
    rows_dev, width = mate.shape
    return pl.pallas_call(
        pack_kernel,
        name="pack",
        out_shape=shape((2 * rows_dev, width + LANES), BF16),
        in_specs=[VMEM] * 3,
        out_specs=VMEM,
        compiler_params=params(4),
        cost_estimate=COST,
    )(own, mate, mate_names)


def normalize_kernel(after_ref, weights_ref, unit_ref, turned_ref, norms_ref):
    del after_ref
    lat_rows, width = weights_ref.shape
    for top in range(0, lat_rows, LANES):
        rows = pl.ds(top, LANES)
        squares = jnp.zeros((LANES, LANES), F32)
        for left in range(0, width, LANES):
            tile = weights_ref[rows, left : left + LANES].astype(F32)
            squares = squares + tile * tile
        norms = jnp.sqrt(jnp.sum(squares, axis=1, keepdims=True) + 1e-06)
        norms_ref[rows, :] = norms
        scale = jnp.broadcast_to(1.0 / norms, (LANES, LANES))
        for left in range(0, width, LANES):
            tile = weights_ref[rows, left : left + LANES].astype(F32)
            unit = (tile * scale).astype(BF16)
            unit_ref[rows, left : left + LANES] = unit
            turned_ref[left : left + LANES, rows] = unit.T


def normalize(after, weights):
    lat_rows, width = weights.shape
    return pl.pallas_call(
        normalize_kernel,
        name="normalize",
        out_shape=(
            shape((lat_rows, width), BF16),
            shape((width, lat_rows), BF16),
            shape((lat_rows, 1), F32),
        ),
        in_specs=[ANY, VMEM],
        out_specs=(VMEM,) * 3,
        compiler_params=params(20),
        cost_estimate=pl.CostEstimate(
            flops=4 * lat_rows * width, bytes_accessed=6 * lat_rows * width, transcendentals=0
        ),
    )(after, weights)


def forward_kernel(rows_dev, top, splits, dec_ref, enc_ref, *refs):
    units, turneds, refs = refs[:splits], refs[splits : 2 * splits], refs[2 * splits :]
    chips = len(refs) - 8
    pieces = restored(ORDER, refs[:chips])
    contrib_ref, cent_ref, input_ref, codes_ref, base_ref, act_ref, hit_ref, rows_ref = refs[chips:]
    count = 2 * chips * rows_dev
    width, lat_rows = units[0].shape[1], base_ref.shape[1]
    for k, piece in enumerate(pieces):
        rows_ref[2 * k * rows_dev : 2 * (k + 1) * rows_dev, :] = piece[...].astype(F32)
    input_ref[...] = rows_ref[:, :width].astype(BF16)
    centered = (rows_ref[:, :width] - dec_ref[...]).astype(BF16)
    cent_ref[...] = centered
    base = times(centered, turneds)
    base_ref[...] = base
    preact = base + enc_ref[...]
    act = jnp.maximum(preact, 0.0) + jnp.log1p(jnp.exp(-jnp.abs(preact)))
    act_ref[...] = act
    first = lax.axis_index("latent") * (lat_rows // BLK)
    lat = lax.broadcasted_iota(jnp.int32, (count, lat_rows), 1)
    block_of = (first + lat // BLK).astype(F32)
    names = rows_ref[:, width:]
    hit = jnp.zeros((count, lat_rows), F32)
    for k in range(top):
        name = names[:, k : k + 1] * RADIX + names[:, top + k : top + k + 1]
        hit = jnp.where(name == block_of, 1.0, hit)
    hit_ref[...] = hit
    codes = (act * hit).astype(BF16)
    codes_ref[...] = codes
    at, contrib = 0, None
    for unit in units:
        part = codes[:, at : at + unit.shape[0]]
        term = jnp.dot(part, unit[...], preferred_element_type=F32)
        contrib = term if contrib is None else contrib + term
        at += unit.shape[0]
    contrib_ref[...] = contrib


def times(x, parts):
    return jnp.concatenate(
        [jnp.dot(x, part[...], preferred_element_type=F32) for part in parts], axis=1
    )


def forward(rows_dev, top, dec, enc, units, turneds, pieces):
    lat_rows, width = enc.shape[1], units[0].shape[1]
    count = 2 * len(pieces) * rows_dev
    return pl.pallas_call(
        functools.partial(forward_kernel, rows_dev, top, len(units)),
        name="forward",
        out_shape=(
            shape((count, width), F32),
            shape((count, width), BF16),
            shape((count, width), BF16),
            shape((count, lat_rows), BF16),
            shape((count, lat_rows), F32),
            shape((count, lat_rows), F32),
            shape((count, lat_rows), F32),
        ),
        in_specs=[VMEM] * (2 + 2 * len(units) + len(pieces)),
        out_specs=(VMEM,) * 7,
        scratch_shapes=[pltpu.VMEM((count, width + LANES), F32)],
        compiler_params=params(20),
        cost_estimate=pl.CostEstimate(
            flops=4 * count * lat_rows * width,
            bytes_accessed=4 * lat_rows * width,
            transcendentals=2 * count * lat_rows,
        ),
    )(dec, enc, *units, *turneds, *taken(ORDER, pieces))


def side_kernel(rows_dev, act_ref, hit_ref, codes_ref, base_ref, enc_ref, *outs):
    scores_ref, gate_ref, second_ref, compact_ref = outs
    count, lat_rows = act_ref.shape
    block_count = lat_rows // BLK
    me = lax.axis_index("latent")
    latent = lax.broadcasted_iota(jnp.int32, (block_count, lat_rows), 1)
    block = lax.broadcasted_iota(jnp.int32, (block_count, lat_rows), 0)
    inside = jnp.where(latent // BLK == block, 1.0 / BLK, 0.0).astype(F32)
    means = lax.dot_general(
        inside,
        act_ref[...],
        (((1,), (1,)), ((), ())),
        preferred_element_type=F32,
        precision=lax.Precision.HIGHEST,
    )
    at = lax.broadcasted_iota(jnp.int32, (count, count), 0)
    place = lax.broadcasted_iota(jnp.int32, (count, count), 1)
    relative = ((place // rows_dev) ^ me) * rows_dev + place % rows_dev
    order = jnp.where(relative == at, 1.0, 0.0).astype(F32)
    scores_ref[...] = jnp.dot(
        means, order, preferred_element_type=F32, precision=lax.Precision.HIGHEST
    )
    hit = hit_ref[...]
    preact = base_ref[...] + enc_ref[...]
    gate_ref[...] = hit * jax.nn.sigmoid(preact)
    earlier = jnp.where(place < at, 1.0, 0.0).astype(BF16)
    before = jnp.dot(earlier, hit.astype(BF16), preferred_element_type=F32)
    second = jnp.where(before == 1.0, hit, 0.0)
    first = jnp.where(before == 0.0, hit, 0.0)
    second_ref[...] = second
    codes = codes_ref[...].astype(F32)
    number = (lax.broadcasted_iota(jnp.int32, (count, lat_rows), 0) + 1).astype(F32)
    rows = []
    for slot in (first, second):
        rows.append(jnp.sum(slot * codes, axis=0, keepdims=True))
    for slot in (first, second):
        rows.append(jnp.sum(slot * number, axis=0, keepdims=True))
    for at, row in enumerate(rows):
        compact_ref[at : at + 1, :] = row


def side(rows_dev, act, hit, codes, base, enc):
    count, lat_rows = act.shape
    return pl.pallas_call(
        functools.partial(side_kernel, rows_dev),
        name="side",
        out_shape=(
            shape((lat_rows // BLK, count), F32),
            shape((count, lat_rows), F32),
            shape((count, lat_rows), F32),
            shape((2 * CAP, lat_rows), F32),
        ),
        in_specs=[VMEM] * 5,
        out_specs=(VMEM,) * 4,
        compiler_params=params(20),
        cost_estimate=pl.CostEstimate(
            flops=8 * count * lat_rows * 64, bytes_accessed=32 * count * lat_rows, transcendentals=0
        ),
    )(act, hit, codes, base, enc)


def exchanged(value, step, mask):
    blocks = range(value.shape[0] // step)
    return jnp.concatenate(
        [value[(k ^ mask) * step : ((k ^ mask) + 1) * step] for k in blocks], axis=0
    )


def combine_kernel(rows_dev, mine_ref, mate_ref, sums_ref, sent_ref):
    sums = mine_ref[...] + exchanged(mate_ref[...], rows_dev, 1)
    sums_ref[...] = sums
    sent_ref[...] = sums.astype(BF16)


def combine(rows_dev, mine, mate):
    return pl.pallas_call(
        functools.partial(combine_kernel, rows_dev),
        name="combine",
        out_shape=(shape(mine.shape, F32), shape(mine.shape, BF16)),
        in_specs=[VMEM] * 2,
        out_specs=(VMEM, VMEM),
        compiler_params=params(12),
    )(mine, mate)


def errors_kernel(rows_dev, dec_ref, input_ref, parts, recon_ref, errors_ref):
    total = parts[0][...]
    for j in range(1, len(parts)):
        total = total + exchanged(parts[j][...].astype(F32), 2 * rows_dev, j)
    full = total + dec_ref[...]
    recon_ref[...] = full[:rows_dev]
    errors_ref[...] = (full - input_ref[...].astype(F32)).astype(BF16)


def backward_kernel(groups, rows_dev, splits, *refs):
    turneds, refs = refs[:splits], refs[splits:]
    cent_ref, codes_ref, base_ref, gate_ref = refs[:4]
    refs = refs[4:]
    second_ref, compact_ref = refs[:2]
    if rows_dev:
        chips = cent_ref.shape[0] // (2 * rows_dev)
        dec_ref, input_ref = refs[2:4]
        parts, outs = restored(ORDER, refs[4 : 4 + chips]), refs[4 + chips :]
        recon_ref, packets, errors_ref = outs[0], outs[1:-1], outs[-1]
        errors_kernel(rows_dev, dec_ref, input_ref, parts, recon_ref, errors_ref)
    else:
        errors_ref, packets = refs[2], refs[3:]
    count, width = cent_ref.shape
    lat_rows = codes_ref.shape[1]
    cols = width // groups
    grad = times(errors_ref[...], turneds)
    pre_grad = (grad * gate_ref[...]).astype(BF16).astype(F32)
    codes = codes_ref[...].astype(F32)
    along = jnp.sum(codes * grad + pre_grad * base_ref[...], axis=0, keepdims=True)
    high = along.astype(BF16).astype(F32)
    both = jnp.sum(pre_grad, axis=0, keepdims=True)
    later = jnp.sum(pre_grad * second_ref[...], axis=0, keepdims=True)
    table = compact_ref[...]
    terms = jnp.concatenate([table, both - later, later, high, along - high], axis=0).astype(BF16)
    group = lax.axis_index("dp")
    for k, packet in enumerate(packets):
        at = pl.ds(pl.multiple_of((group ^ k) * cols, LANES), cols)
        packet[:count, :] = errors_ref[:, at]
        packet[count : 2 * count, :] = cent_ref[:, at]
        for part in range(lat_rows // cols):
            rows = pl.ds(2 * count + part * TERMS, TERMS)
            packet[rows, :] = terms[:, part * cols : (part + 1) * cols]


def backward(groups, rows_dev, turneds, cent, rest):
    count, width = cent.shape
    lat_rows = rest[0].shape[1]
    cols = width // groups
    packet = shape((2 * count + TERMS * lat_rows // cols, cols), BF16)
    outs = (packet,) * groups
    scratch = []
    if rows_dev:
        outs = (shape((rows_dev, width), F32),) + outs
        scratch = [pltpu.VMEM((count, width), BF16)]
    return pl.pallas_call(
        functools.partial(backward_kernel, groups, rows_dev, len(turneds)),
        name="backward",
        out_shape=outs,
        in_specs=[VMEM] * (len(turneds) + 1 + len(rest)),
        out_specs=(VMEM,) * len(outs),
        scratch_shapes=scratch,
        compiler_params=params(20),
        cost_estimate=pl.CostEstimate(
            flops=2 * count * lat_rows * width, bytes_accessed=2 * lat_rows * width, transcendentals=0
        ),
    )(*turneds, cent, *rest)


def rounded_kernel(value_ref, out_ref):
    out_ref[...] = value_ref[...].astype(BF16)


def rounded(value):
    return pl.pallas_call(
        rounded_kernel,
        name="rounded",
        out_shape=shape(value.shape, BF16),
        in_specs=[VMEM],
        out_specs=VMEM,
        compiler_params=params(4),
    )(value)


def gradient_kernel(count, splits, *refs):
    units, norms, refs = refs[:splits], refs[splits : 2 * splits], refs[2 * splits :]
    out_ref, left_ref, right_ref, held_ref, sems = refs[-5:]
    packets = restored(ORDER_DP, refs[:-5])
    lat_rows, cols = out_ref.shape
    along = jnp.zeros((1, lat_rows), F32)
    number = (lax.broadcasted_iota(jnp.int32, (count, lat_rows), 0) + 1).astype(F32)
    for g, packet in enumerate(packets):
        base = g * 2 * count
        right_ref[base : base + 2 * count, :] = packet[: 2 * count, :]
        parts = [
            packet[2 * count + p * TERMS : 2 * count + (p + 1) * TERMS, :].astype(F32)
            for p in range(lat_rows // cols)
        ]
        terms = jnp.concatenate(parts, axis=1)
        code0, code1, row0, row1, grad0, grad1, high, low = [
            terms[t : t + 1] for t in range(TERMS)
        ]
        at0, at1 = number == row0, number == row1
        code = jnp.where(at0, code0, jnp.where(at1, code1, 0.0))
        grad = jnp.where(at0, grad0, jnp.where(at1, grad1, 0.0))
        left_ref[base : base + count, :] = code.astype(BF16)
        left_ref[base + count : base + 2 * count, :] = grad.astype(BF16)
        along = along + (high + low)
    start = pl.multiple_of(lax.axis_index("dp") * cols, LANES)
    copies = []
    which, first = 0, 0
    for at in range(lat_rows // LANES):
        if at * LANES == first + units[which].shape[0]:
            first, which = at * LANES, which + 1
        rows = pl.ds(at * LANES, LANES)
        outer = lax.dot_general(
            left_ref[:, rows],
            right_ref[...],
            (((0,), (0,)), ((), ())),
            preferred_element_type=F32,
        )
        column = jnp.broadcast_to(along[:, at * LANES : (at + 1) * LANES], (LANES, LANES)).T
        part = pl.ds(at * LANES - first, LANES)
        unit = units[which][part, pl.ds(start, cols)].astype(F32)
        inverse = 1.0 / norms[which][part, :]
        held_ref[rows, :] = (outer - unit * column[:, :1]) * inverse
        copies.append(pltpu.make_async_copy(held_ref.at[rows], out_ref.at[rows], sems.at[at]))
        copies[-1].start()
    for copy in copies:
        copy.wait()


def gradient(count, units, norms, packets):
    lat_rows = sum(unit.shape[0] for unit in units)
    cols = packets[0].shape[1]
    depth = 2 * count * len(packets)
    return pl.pallas_call(
        functools.partial(gradient_kernel, count, len(units)),
        name="gradient",
        out_shape=shape((lat_rows, cols), F32),
        in_specs=[VMEM] * (2 * len(units) + len(packets)),
        out_specs=HBM,
        scratch_shapes=[
            pltpu.VMEM((depth, lat_rows), BF16),
            pltpu.VMEM((depth, cols), BF16),
            pltpu.VMEM((lat_rows, cols), F32),
            pltpu.SemaphoreType.DMA((lat_rows // LANES,)),
        ],
        compiler_params=params(24),
        cost_estimate=pl.CostEstimate(
            flops=2 * depth * lat_rows * cols, bytes_accessed=8 * lat_rows * cols, transcendentals=0
        ),
    )(*units, *norms, *taken(ORDER_DP, packets))


def local(inputs, blocks, weights, enc_bias, dec_bias):
    rows_dev = inputs.shape[0]
    top = blocks.shape[1]
    chips = lax.axis_size("latent") // 2
    groups = lax.axis_size("dp")
    count = 2 * chips * rows_dev
    dec, enc = dec_bias[None, :], enc_bias[None, :]

    mate, mate_names = swap(inputs, "latent", 1), swap(blocks, "latent", 1)
    width = inputs.shape[1]
    lane = lax.broadcasted_iota(jnp.int32, (rows_dev, width + LANES), 1)
    high = jnp.pad(blocks, ((0, 0), (width, LANES - top)))
    low = jnp.pad(blocks, ((0, 0), (width + top, LANES - 2 * top)))
    lists = jnp.where(lane < width + top, high >> SHIFT, low & (RADIX - 1))
    own = jnp.where(lane < width, jnp.pad(inputs, ((0, 0), (0, LANES))), lists.astype(BF16))
    both = pack(own, mate, mate_names)
    pieces = swaps([both] * chips, "latent", 2)
    units, turneds, norms = ([x] for x in normalize(both, weights))
    contrib, cent, rows, codes, base, act, hit = forward(
        rows_dev, top, dec, enc, units, turneds, pieces
    )
    sums, sent = combine(rows_dev, contrib, swap(contrib, "latent", 1))
    block_scores, gate, second, compact = side(rows_dev, act, hit, codes, base, enc)
    known = (codes, base, gate, second, compact)
    if chips <= DIRECT:
        parts = [sums] + swaps([sent] * chips, "latent", 2)[1:]
        recon, *packets = backward(
            groups, rows_dev, turneds, cent, (*known, dec, rows, *taken(ORDER, parts))
        )
    else:
        full = dec_bias + sums[:rows_dev]
        for j in range(1, chips):
            at = 2 * j * rows_dev
            full = full + swap(sums[at : at + rows_dev], "latent", 2 * j)
        recon = full
        errors = (full - rows[:rows_dev].astype(F32)).astype(BF16)
        errors = jnp.concatenate([errors, swap(errors, "latent", 1)], axis=0)
        errors = jnp.concatenate(swaps([errors] * chips, "latent", 2), axis=0)
        packets = backward(groups, 0, turneds, cent, (*known, errors))
    packets = swaps(packets, "dp", 1)
    grad_weights = gradient(count, units, norms, packets)
    return (rounded(recon), grad_weights, block_scores)


def solution(mesh):
    in_specs = (
        P(("dp", "latent"), None),
        P(("dp", "latent"), None),
        P("latent", None),
        P("latent"),
        P(),
    )
    out_specs = (P(("dp", "latent"), None), P("latent", "dp"), P("latent", "dp"))
    return jax.shard_map(local, mesh=mesh, in_specs=in_specs, out_specs=out_specs, check_vma=False)
```

```python
import functools

import jax
import jax.numpy as jnp
from jax import lax
from jax.experimental import pallas as pl
from jax.experimental.pallas import tpu as pltpu
from jax.sharding import PartitionSpec as P

BLK = 64
CAP = 2
SHIFT = 5
RADIX = 1 << SHIFT
LANES = 128
DIRECT = 4
TERMS = 8
ORDER = (0, 1, 2, 3)
LATE = 2
VMEM = pl.BlockSpec(memory_space=pltpu.VMEM)
HBM = pl.BlockSpec(memory_space=pltpu.MemorySpace.HBM)
ANY = pl.BlockSpec(memory_space=pl.ANY)
F32, BF16 = jnp.float32, jnp.bfloat16
COST = pl.CostEstimate(flops=2**34, bytes_accessed=16 * 2**20, transcendentals=2**24)


def swap(x, axis, mask):
    size = lax.axis_size(axis)
    return lax.ppermute(x, axis, [(i, i ^ mask) for i in range(size)])


def swaps(xs, axis, step):
    return [swap(x, axis, step * k) if k else x for k, x in enumerate(xs)]


def taken(order, xs):
    return tuple(xs[k] for k in ranked(order, len(xs)))


def ranked(order, count):
    return order if len(order) == count else tuple(range(count))


def restored(order, refs):
    order = ranked(order, len(refs))
    return [refs[order.index(k)] for k in range(len(refs))]


def params(mib):
    return pltpu.CompilerParams(vmem_limit_bytes=mib * 2**20)


def shape(dims, dtype):
    return jax.ShapeDtypeStruct(dims, dtype)


def pack_kernel(own_ref, mate_ref, mate_names_ref, out_ref):
    rows_dev, width = mate_ref.shape
    lane = lax.broadcasted_iota(jnp.int32, (rows_dev, LANES), 1)
    out_ref[:rows_dev, :] = own_ref[...]
    out_ref[rows_dev:, :width] = mate_ref[...]
    out_ref[rows_dev:, width:] = coded(mate_names_ref[...], lane).astype(F32).astype(BF16)


def coded(names, lane):
    top = names.shape[1]
    value = jnp.zeros(lane.shape, jnp.int32)
    for k in range(top):
        name = names[:, k : k + 1]
        value = jnp.where(lane == k, name // RADIX, value)
        value = jnp.where(lane == top + k, name % RADIX, value)
    return value


def pack(own, mate, mate_names):
    rows_dev, width = mate.shape
    return pl.pallas_call(
        pack_kernel,
        name="pack",
        out_shape=shape((2 * rows_dev, width + LANES), BF16),
        in_specs=[VMEM] * 3,
        out_specs=VMEM,
        compiler_params=params(4),
        cost_estimate=COST,
    )(own, mate, mate_names)


def normalize_kernel(after_ref, weights_ref, unit_ref, turned_ref, inverse_ref):
    del after_ref
    lat_rows, width = weights_ref.shape
    for top in range(0, lat_rows, LANES):
        rows = pl.ds(top, LANES)
        squares = jnp.zeros((LANES, LANES), F32)
        for left in range(0, width, LANES):
            tile = weights_ref[rows, left : left + LANES].astype(F32)
            squares = squares + tile * tile
        norms = jnp.sqrt(jnp.sum(squares, axis=1, keepdims=True) + 1e-06)
        scale = jnp.broadcast_to(1.0 / norms, (LANES, LANES))
        inverse_ref[rows, :] = scale
        for left in range(0, width, LANES):
            tile = weights_ref[rows, left : left + LANES].astype(F32)
            unit = (tile * scale).astype(BF16)
            unit_ref[rows, left : left + LANES] = unit
            turned_ref[left : left + LANES, rows] = unit.T


def normalize(after, weights):
    lat_rows, width = weights.shape
    return pl.pallas_call(
        normalize_kernel,
        name="normalize",
        out_shape=(
            shape((lat_rows, width), BF16),
            shape((width, lat_rows), BF16),
            shape((lat_rows, LANES), F32),
        ),
        in_specs=[ANY, VMEM],
        out_specs=(VMEM,) * 3,
        compiler_params=params(20),
        cost_estimate=pl.CostEstimate(
            flops=4 * lat_rows * width, bytes_accessed=6 * lat_rows * width, transcendentals=0
        ),
    )(after, weights)


def forward_kernel(rows_dev, top, splits, dec_ref, enc_ref, *refs):
    units, turneds, refs = refs[:splits], refs[splits : 2 * splits], refs[2 * splits :]
    chips = len(refs) - 8
    pieces = restored(ORDER, refs[:chips])
    contrib_ref, cent_ref, input_ref, codes_ref, base_ref, act_ref, hit_ref, rows_ref = refs[chips:]
    count = 2 * chips * rows_dev
    width, lat_rows = units[0].shape[1], base_ref.shape[1]
    for k, piece in enumerate(pieces):
        rows_ref[2 * k * rows_dev : 2 * (k + 1) * rows_dev, :] = piece[...].astype(F32)
    input_ref[...] = rows_ref[:, :width].astype(BF16)
    centered = (rows_ref[:, :width] - dec_ref[...]).astype(BF16)
    cent_ref[...] = centered
    base = times(centered, turneds)
    base_ref[...] = base
    preact = base + enc_ref[...]
    act = jnp.maximum(preact, 0.0) + jnp.log1p(jnp.exp(-jnp.abs(preact)))
    act_ref[...] = act
    first = lax.axis_index("latent") * (lat_rows // BLK)
    lat = lax.broadcasted_iota(jnp.int32, (count, lat_rows), 1)
    block_of = (first + lat // BLK).astype(F32)
    names = rows_ref[:, width:]
    hit = jnp.zeros((count, lat_rows), F32)
    for k in range(top):
        name = names[:, k : k + 1] * RADIX + names[:, top + k : top + k + 1]
        hit = jnp.where(name == block_of, 1.0, hit)
    hit_ref[...] = hit
    codes = (act * hit).astype(BF16)
    codes_ref[...] = codes
    at, contrib = 0, None
    for unit in units:
        part = codes[:, at : at + unit.shape[0]]
        term = jnp.dot(part, unit[...], preferred_element_type=F32)
        contrib = term if contrib is None else contrib + term
        at += unit.shape[0]
    contrib_ref[...] = contrib


def times(x, parts):
    return jnp.concatenate(
        [jnp.dot(x, part[...], preferred_element_type=F32) for part in parts], axis=1
    )


def forward(rows_dev, top, dec, enc, units, turneds, pieces):
    lat_rows, width = enc.shape[1], units[0].shape[1]
    count = 2 * len(pieces) * rows_dev
    return pl.pallas_call(
        functools.partial(forward_kernel, rows_dev, top, len(units)),
        name="forward",
        out_shape=(
            shape((count, width), F32),
            shape((count, width), BF16),
            shape((count, width), BF16),
            shape((count, lat_rows), BF16),
            shape((count, lat_rows), F32),
            shape((count, lat_rows), F32),
            shape((count, lat_rows), F32),
        ),
        in_specs=[VMEM] * (2 + 2 * len(units) + len(pieces)),
        out_specs=(VMEM,) * 7,
        scratch_shapes=[pltpu.VMEM((count, width + LANES), F32)],
        compiler_params=params(20),
        cost_estimate=pl.CostEstimate(
            flops=4 * count * lat_rows * width,
            bytes_accessed=4 * lat_rows * width,
            transcendentals=2 * count * lat_rows,
        ),
    )(dec, enc, *units, *turneds, *taken(ORDER, pieces))


def side_kernel(rows_dev, act_ref, hit_ref, codes_ref, base_ref, enc_ref, *outs):
    scores_ref, gate_ref, second_ref, compact_ref = outs
    count, lat_rows = act_ref.shape
    block_count = lat_rows // BLK
    me = lax.axis_index("latent")
    latent = lax.broadcasted_iota(jnp.int32, (block_count, lat_rows), 1)
    block = lax.broadcasted_iota(jnp.int32, (block_count, lat_rows), 0)
    inside = jnp.where(latent // BLK == block, 1.0 / BLK, 0.0).astype(F32)
    means = lax.dot_general(
        inside,
        act_ref[...],
        (((1,), (1,)), ((), ())),
        preferred_element_type=F32,
        precision=lax.Precision.HIGHEST,
    )
    at = lax.broadcasted_iota(jnp.int32, (count, count), 0)
    place = lax.broadcasted_iota(jnp.int32, (count, count), 1)
    relative = ((place // rows_dev) ^ me) * rows_dev + place % rows_dev
    order = jnp.where(relative == at, 1.0, 0.0).astype(F32)
    scores_ref[...] = jnp.dot(
        means, order, preferred_element_type=F32, precision=lax.Precision.HIGHEST
    )
    hit = hit_ref[...]
    preact = base_ref[...] + enc_ref[...]
    gate_ref[...] = hit * jax.nn.sigmoid(preact)
    earlier = jnp.where(place < at, 1.0, 0.0).astype(BF16)
    before = jnp.dot(earlier, hit.astype(BF16), preferred_element_type=F32)
    second = jnp.where(before == 1.0, hit, 0.0)
    first = jnp.where(before == 0.0, hit, 0.0)
    second_ref[...] = second
    codes = codes_ref[...].astype(F32)
    number = (lax.broadcasted_iota(jnp.int32, (count, lat_rows), 0) + 1).astype(F32)
    rows = []
    for slot in (first, second):
        rows.append(jnp.sum(slot * codes, axis=0, keepdims=True))
    for slot in (first, second):
        rows.append(jnp.sum(slot * number, axis=0, keepdims=True))
    for at, row in enumerate(rows):
        compact_ref[at : at + 1, :] = row


def side(rows_dev, act, hit, codes, base, enc):
    count, lat_rows = act.shape
    return pl.pallas_call(
        functools.partial(side_kernel, rows_dev),
        name="side",
        out_shape=(
            shape((lat_rows // BLK, count), F32),
            shape((count, lat_rows), F32),
            shape((count, lat_rows), F32),
            shape((2 * CAP, lat_rows), F32),
        ),
        in_specs=[VMEM] * 5,
        out_specs=(VMEM,) * 4,
        compiler_params=params(20),
        cost_estimate=pl.CostEstimate(
            flops=8 * count * lat_rows * 64, bytes_accessed=32 * count * lat_rows, transcendentals=0
        ),
    )(act, hit, codes, base, enc)


def exchanged(value, step, mask):
    blocks = range(value.shape[0] // step)
    return jnp.concatenate(
        [value[(k ^ mask) * step : ((k ^ mask) + 1) * step] for k in blocks], axis=0
    )


def combine_kernel(rows_dev, mine_ref, mate_ref, sums_ref, sent_ref):
    sums = mine_ref[...] + exchanged(mate_ref[...], rows_dev, 1)
    sums_ref[...] = sums
    sent_ref[...] = sums.astype(BF16)


def combine(rows_dev, mine, mate):
    return pl.pallas_call(
        functools.partial(combine_kernel, rows_dev),
        name="combine",
        out_shape=(shape(mine.shape, F32), shape(mine.shape, BF16)),
        in_specs=[VMEM] * 2,
        out_specs=(VMEM, VMEM),
        compiler_params=params(12),
    )(mine, mate)


def errors_kernel(rows_dev, dec_ref, input_ref, parts, recon_ref, errors_ref):
    total = parts[0][...]
    for j in range(1, len(parts)):
        total = total + exchanged(parts[j][...].astype(F32), 2 * rows_dev, j)
    full = total + dec_ref[...]
    recon_ref[...] = full[:rows_dev]
    errors_ref[...] = (full - input_ref[...].astype(F32)).astype(BF16)


def backward_kernel(groups, rows_dev, splits, *refs):
    turneds, refs = refs[:splits], refs[splits:]
    cent_ref, codes_ref, base_ref, gate_ref = refs[:4]
    refs = refs[4:]
    second_ref, compact_ref = refs[:2]
    if rows_dev:
        chips = cent_ref.shape[0] // (2 * rows_dev)
        dec_ref, input_ref = refs[2:4]
        parts, outs = restored(ORDER, refs[4 : 4 + chips]), refs[4 + chips :]
        recon_ref, packets, errors_ref = outs[0], outs[1:-1], outs[-1]
        errors_kernel(rows_dev, dec_ref, input_ref, parts, recon_ref, errors_ref)
    else:
        errors_ref, packets = refs[2], refs[3:]
    count, width = cent_ref.shape
    lat_rows = codes_ref.shape[1]
    cols = width // groups
    grad = times(errors_ref[...], turneds)
    pre_grad = (grad * gate_ref[...]).astype(BF16).astype(F32)
    codes = codes_ref[...].astype(F32)
    along = jnp.sum(codes * grad + pre_grad * base_ref[...], axis=0, keepdims=True)
    high = along.astype(BF16).astype(F32)
    both = jnp.sum(pre_grad, axis=0, keepdims=True)
    later = jnp.sum(pre_grad * second_ref[...], axis=0, keepdims=True)
    table = compact_ref[...]
    terms = jnp.concatenate([table, both - later, later, high, along - high], axis=0).astype(BF16)
    group = lax.axis_index("dp")
    for k, packet in enumerate(packets):
        at = pl.ds(pl.multiple_of((group ^ k) * cols, LANES), cols)
        packet[:count, :] = errors_ref[:, at]
        packet[count : 2 * count, :] = cent_ref[:, at]
        for part in range(lat_rows // cols):
            rows = pl.ds(2 * count + part * TERMS, TERMS)
            packet[rows, :] = terms[:, part * cols : (part + 1) * cols]


def backward(groups, rows_dev, turneds, cent, rest):
    count, width = cent.shape
    lat_rows = rest[0].shape[1]
    cols = width // groups
    packet = shape((2 * count + TERMS * lat_rows // cols, cols), BF16)
    outs = (packet,) * groups
    scratch = []
    if rows_dev:
        outs = (shape((rows_dev, width), F32),) + outs
        scratch = [pltpu.VMEM((count, width), BF16)]
    return pl.pallas_call(
        functools.partial(backward_kernel, groups, rows_dev, len(turneds)),
        name="backward",
        out_shape=outs,
        in_specs=[VMEM] * (len(turneds) + 1 + len(rest)),
        out_specs=(VMEM,) * len(outs),
        scratch_shapes=scratch,
        compiler_params=params(20),
        cost_estimate=pl.CostEstimate(
            flops=2 * count * lat_rows * width, bytes_accessed=2 * lat_rows * width, transcendentals=0
        ),
    )(*turneds, cent, *rest)


def rounded_kernel(value_ref, out_ref):
    out_ref[...] = value_ref[...].astype(BF16)


def rounded(value):
    return pl.pallas_call(
        rounded_kernel,
        name="rounded",
        out_shape=shape(value.shape, BF16),
        in_specs=[VMEM],
        out_specs=VMEM,
        compiler_params=params(4),
    )(value)


def gradient_kernel(count, given, unit_ref, inverse_ref, *refs):
    out_ref, left_ref, right_ref, held_ref, sems = refs[-5:]
    packets, before_refs = refs[:given], refs[given:-5]
    lat_rows, cols = out_ref.shape
    depth = 2 * count * len(packets)
    extra = left_ref.shape[0] - depth
    along = []
    number = (lax.broadcasted_iota(jnp.int32, (count, lat_rows), 0) + 1).astype(F32)
    for g, packet in enumerate(packets):
        base = g * 2 * count
        right_ref[base : base + 2 * count, :cols] = packet[: 2 * count, :]
        parts = [
            packet[2 * count + p * TERMS : 2 * count + (p + 1) * TERMS, :].astype(F32)
            for p in range(lat_rows // cols)
        ]
        terms = jnp.concatenate(parts, axis=1)
        code0, code1, row0, row1, grad0, grad1 = [terms[t : t + 1] for t in range(TERMS - 2)]
        at0, at1 = number == row0, number == row1
        code = jnp.where(at0, code0, jnp.where(at1, code1, 0.0))
        grad = jnp.where(at0, grad0, jnp.where(at1, grad1, 0.0))
        left_ref[base : base + count, :] = code.astype(BF16)
        left_ref[base + count : base + 2 * count, :] = grad.astype(BF16)
        along.append(terms[TERMS - 2 :])
    if extra > 2 * len(packets):
        along.append(jnp.zeros((extra - 2 * len(packets), lat_rows), F32))
    left_ref[depth:, :] = jnp.concatenate(along, axis=0).astype(BF16)
    right_ref[depth:, :cols] = jnp.zeros((extra, cols), BF16)
    right_ref[:depth, cols:] = jnp.zeros((depth, LANES), BF16)
    right_ref[depth:, cols:] = jnp.ones((extra, LANES), BF16)
    start = pl.multiple_of(lax.axis_index("dp") * cols, LANES)
    copies = []
    for at in range(lat_rows // LANES):
        rows = pl.ds(at * LANES, LANES)
        outer = lax.dot_general(
            left_ref[:, rows],
            right_ref[...],
            (((0,), (0,)), ((), ())),
            preferred_element_type=F32,
        )
        unit = unit_ref[rows, pl.ds(start, cols)].astype(F32)
        inverse, total = inverse_ref[rows, :], outer[:, cols:]
        for tile in range(0, cols, LANES):
            part = slice(tile, tile + LANES)
            value = (outer[:, part] - unit[:, part] * total) * inverse
            if before_refs:
                held_ref[rows, part] = before_refs[0][rows, part] + value
            else:
                out_ref[rows, part] = value
        if before_refs:
            copies.append(pltpu.make_async_copy(held_ref.at[rows], out_ref.at[rows], sems.at[at]))
            copies[-1].start()
    for copy in copies:
        copy.wait()


def gradient(name, count, unit, inverse, packets, before):
    lat_rows = unit.shape[0]
    cols = packets[0].shape[1]
    depth = 2 * count * len(packets)
    rows = depth + max(16, 2 * len(packets))
    return pl.pallas_call(
        functools.partial(gradient_kernel, count, len(packets)),
        name=name,
        out_shape=shape((lat_rows, cols), F32),
        in_specs=[VMEM] * (2 + len(packets) + len(before)),
        out_specs=HBM if before else VMEM,
        scratch_shapes=[
            pltpu.VMEM((rows, lat_rows), BF16),
            pltpu.VMEM((rows, cols + LANES), BF16),
            pltpu.VMEM((lat_rows, cols) if before else (8, LANES), F32),
            pltpu.SemaphoreType.DMA((lat_rows // LANES,)),
        ],
        compiler_params=params(24),
        cost_estimate=pl.CostEstimate(
            flops=2 * depth * lat_rows * cols, bytes_accessed=8 * lat_rows * cols, transcendentals=0
        ),
    )(unit, inverse, *packets, *before)


def local(inputs, blocks, weights, enc_bias, dec_bias):
    rows_dev = inputs.shape[0]
    top = blocks.shape[1]
    chips = lax.axis_size("latent") // 2
    groups = lax.axis_size("dp")
    count = 2 * chips * rows_dev
    dec, enc = dec_bias[None, :], enc_bias[None, :]

    mate, mate_names = swap(inputs, "latent", 1), swap(blocks, "latent", 1)
    width = inputs.shape[1]
    lane = lax.broadcasted_iota(jnp.int32, (rows_dev, width + LANES), 1)
    high = jnp.pad(blocks, ((0, 0), (width, LANES - top)))
    low = jnp.pad(blocks, ((0, 0), (width + top, LANES - 2 * top)))
    lists = jnp.where(lane < width + top, high >> SHIFT, low & (RADIX - 1))
    own = jnp.where(lane < width, jnp.pad(inputs, ((0, 0), (0, LANES))), lists.astype(BF16))
    both = pack(own, mate, mate_names)
    pieces = swaps([both] * chips, "latent", 2)
    unit, turned, inverse = normalize(both, weights)
    units, turneds = [unit], [turned]
    contrib, cent, rows, codes, base, act, hit = forward(
        rows_dev, top, dec, enc, units, turneds, pieces
    )
    sums, sent = combine(rows_dev, contrib, swap(contrib, "latent", 1))
    block_scores, gate, second, compact = side(rows_dev, act, hit, codes, base, enc)
    known = (codes, base, gate, second, compact)
    if chips <= DIRECT:
        parts = [sums] + swaps([sent] * chips, "latent", 2)[1:]
        recon, *packets = backward(
            groups, rows_dev, turneds, cent, (*known, dec, rows, *taken(ORDER, parts))
        )
    else:
        full = dec_bias + sums[:rows_dev]
        for j in range(1, chips):
            at = 2 * j * rows_dev
            full = full + swap(sums[at : at + rows_dev], "latent", 2 * j)
        recon = full
        errors = (full - rows[:rows_dev].astype(F32)).astype(BF16)
        errors = jnp.concatenate([errors, swap(errors, "latent", 1)], axis=0)
        errors = jnp.concatenate(swaps([errors] * chips, "latent", 2), axis=0)
        packets = backward(groups, 0, turneds, cent, (*known, errors))
    packets = swaps(packets, "dp", 1)
    late = LATE if groups == len(ORDER) else groups - 1
    early = [p for k, p in enumerate(packets) if k != late]
    partial = gradient("early", count, unit, inverse, early, [])
    grad_weights = gradient("gradient", count, unit, inverse, [packets[late]], [partial])
    return (rounded(recon), grad_weights, block_scores)


def solution(mesh):
    in_specs = (
        P(("dp", "latent"), None),
        P(("dp", "latent"), None),
        P("latent", None),
        P("latent"),
        P(),
    )
    out_specs = (P(("dp", "latent"), None), P("latent", "dp"), P("latent", "dp"))
    return jax.shard_map(local, mesh=mesh, in_specs=in_specs, out_specs=out_specs, check_vma=False)
```

```python
import functools

import jax
import jax.numpy as jnp
from jax import lax
from jax.experimental import pallas as pl
from jax.experimental.pallas import tpu as pltpu
from jax.sharding import PartitionSpec as P

BLK = 64
CAP = 2
SHIFT = 5
RADIX = 1 << SHIFT
LANES = 128
DIRECT = 4
TERMS = 4
ORDER = (0, 1, 2, 3)
LATE = 1
VMEM = pl.BlockSpec(memory_space=pltpu.VMEM)
HBM = pl.BlockSpec(memory_space=pltpu.MemorySpace.HBM)
ANY = pl.BlockSpec(memory_space=pl.ANY)
F32, BF16 = jnp.float32, jnp.bfloat16
COST = pl.CostEstimate(flops=2**34, bytes_accessed=16 * 2**20, transcendentals=2**24)


def swap(x, axis, mask):
    size = lax.axis_size(axis)
    return lax.ppermute(x, axis, [(i, i ^ mask) for i in range(size)])


def swaps(xs, axis, step):
    return [swap(x, axis, step * k) if k else x for k, x in enumerate(xs)]


def taken(order, xs):
    return tuple(xs[k] for k in ranked(order, len(xs)))


def ranked(order, count):
    return order if len(order) == count else tuple(range(count))


def restored(order, refs):
    order = ranked(order, len(refs))
    return [refs[order.index(k)] for k in range(len(refs))]


def params(mib):
    return pltpu.CompilerParams(vmem_limit_bytes=mib * 2**20)


def shape(dims, dtype):
    return jax.ShapeDtypeStruct(dims, dtype)


def pack_kernel(own_ref, mate_ref, mate_names_ref, out_ref):
    rows_dev, width = mate_ref.shape
    lane = lax.broadcasted_iota(jnp.int32, (rows_dev, LANES), 1)
    out_ref[:rows_dev, :] = own_ref[...]
    out_ref[rows_dev:, :width] = mate_ref[...]
    out_ref[rows_dev:, width:] = coded(mate_names_ref[...], lane).astype(F32).astype(BF16)


def coded(names, lane):
    top = names.shape[1]
    value = jnp.zeros(lane.shape, jnp.int32)
    for k in range(top):
        name = names[:, k : k + 1]
        value = jnp.where(lane == k, name // RADIX, value)
        value = jnp.where(lane == top + k, name % RADIX, value)
    return value


def pack(own, mate, mate_names):
    rows_dev, width = mate.shape
    return pl.pallas_call(
        pack_kernel,
        name="pack",
        out_shape=shape((2 * rows_dev, width + LANES), BF16),
        in_specs=[VMEM] * 3,
        out_specs=VMEM,
        compiler_params=params(4),
        cost_estimate=COST,
    )(own, mate, mate_names)


def normalize_kernel(after_ref, weights_ref, unit_ref, turned_ref, inverse_ref):
    del after_ref
    lat_rows, width = weights_ref.shape
    for top in range(0, lat_rows, LANES):
        rows = pl.ds(top, LANES)
        squares = jnp.zeros((LANES, LANES), F32)
        for left in range(0, width, LANES):
            tile = weights_ref[rows, left : left + LANES].astype(F32)
            squares = squares + tile * tile
        norms = jnp.sqrt(jnp.sum(squares, axis=1, keepdims=True) + 1e-06)
        scale = jnp.broadcast_to(1.0 / norms, (LANES, LANES))
        inverse_ref[rows, :] = scale
        for left in range(0, width, LANES):
            tile = weights_ref[rows, left : left + LANES].astype(F32)
            unit = (tile * scale).astype(BF16)
            unit_ref[rows, left : left + LANES] = unit
            turned_ref[left : left + LANES, rows] = unit.T


def normalize(after, weights):
    lat_rows, width = weights.shape
    return pl.pallas_call(
        normalize_kernel,
        name="normalize",
        out_shape=(
            shape((lat_rows, width), BF16),
            shape((width, lat_rows), BF16),
            shape((lat_rows, LANES), F32),
        ),
        in_specs=[ANY, VMEM],
        out_specs=(VMEM,) * 3,
        compiler_params=params(20),
        cost_estimate=pl.CostEstimate(
            flops=4 * lat_rows * width, bytes_accessed=6 * lat_rows * width, transcendentals=0
        ),
    )(after, weights)


def forward_kernel(rows_dev, top, splits, dec_ref, enc_ref, *refs):
    units, turneds, refs = refs[:splits], refs[splits : 2 * splits], refs[2 * splits :]
    chips = len(refs) - 8
    pieces = restored(ORDER, refs[:chips])
    contrib_ref, cent_ref, input_ref, codes_ref, base_ref, act_ref, hit_ref, rows_ref = refs[chips:]
    count = 2 * chips * rows_dev
    width, lat_rows = units[0].shape[1], base_ref.shape[1]
    for k, piece in enumerate(pieces):
        rows_ref[2 * k * rows_dev : 2 * (k + 1) * rows_dev, :] = piece[...].astype(F32)
    input_ref[...] = rows_ref[:, :width].astype(BF16)
    centered = (rows_ref[:, :width] - dec_ref[...]).astype(BF16)
    cent_ref[...] = centered
    base = times(centered, turneds)
    base_ref[...] = base
    preact = base + enc_ref[...]
    act = jnp.maximum(preact, 0.0) + jnp.log1p(jnp.exp(-jnp.abs(preact)))
    act_ref[...] = act
    first = lax.axis_index("latent") * (lat_rows // BLK)
    lat = lax.broadcasted_iota(jnp.int32, (count, lat_rows), 1)
    block_of = (first + lat // BLK).astype(F32)
    names = rows_ref[:, width:]
    hit = jnp.zeros((count, lat_rows), F32)
    for k in range(top):
        name = names[:, k : k + 1] * RADIX + names[:, top + k : top + k + 1]
        hit = jnp.where(name == block_of, 1.0, hit)
    hit_ref[...] = hit
    codes = (act * hit).astype(BF16)
    codes_ref[...] = codes
    at, contrib = 0, None
    for unit in units:
        part = codes[:, at : at + unit.shape[0]]
        term = jnp.dot(part, unit[...], preferred_element_type=F32)
        contrib = term if contrib is None else contrib + term
        at += unit.shape[0]
    contrib_ref[...] = contrib


def times(x, parts):
    return jnp.concatenate(
        [jnp.dot(x, part[...], preferred_element_type=F32) for part in parts], axis=1
    )


def forward(rows_dev, top, dec, enc, units, turneds, pieces):
    lat_rows, width = enc.shape[1], units[0].shape[1]
    count = 2 * len(pieces) * rows_dev
    return pl.pallas_call(
        functools.partial(forward_kernel, rows_dev, top, len(units)),
        name="forward",
        out_shape=(
            shape((count, width), F32),
            shape((count, width), BF16),
            shape((count, width), BF16),
            shape((count, lat_rows), BF16),
            shape((count, lat_rows), F32),
            shape((count, lat_rows), F32),
            shape((count, lat_rows), F32),
        ),
        in_specs=[VMEM] * (2 + 2 * len(units) + len(pieces)),
        out_specs=(VMEM,) * 7,
        scratch_shapes=[pltpu.VMEM((count, width + LANES), F32)],
        compiler_params=params(20),
        cost_estimate=pl.CostEstimate(
            flops=4 * count * lat_rows * width,
            bytes_accessed=4 * lat_rows * width,
            transcendentals=2 * count * lat_rows,
        ),
    )(dec, enc, *units, *turneds, *taken(ORDER, pieces))


def side_kernel(groups, hit_ref, codes_ref, base_ref, enc_ref, cent_ref, *outs):
    gate_ref, second_ref, packets = outs[0], outs[1], outs[2:]
    count, lat_rows = hit_ref.shape
    hit = hit_ref[...]
    preact = base_ref[...] + enc_ref[...]
    gate_ref[...] = hit * jax.nn.sigmoid(preact)
    at = lax.broadcasted_iota(jnp.int32, (count, count), 0)
    place = lax.broadcasted_iota(jnp.int32, (count, count), 1)
    earlier = jnp.where(place < at, 1.0, 0.0).astype(BF16)
    before = jnp.dot(earlier, hit.astype(BF16), preferred_element_type=F32)
    second = jnp.where(before == 1.0, hit, 0.0)
    first = jnp.where(before == 0.0, hit, 0.0)
    second_ref[...] = second
    codes = codes_ref[...].astype(F32)
    number = (lax.broadcasted_iota(jnp.int32, (count, lat_rows), 0) + 1).astype(F32)
    terms = [jnp.sum(slot * codes, axis=0, keepdims=True) for slot in (first, second)]
    terms += [jnp.sum(slot * number, axis=0, keepdims=True) for slot in (first, second)]
    fill(groups, packets, cent_ref, jnp.concatenate(terms, axis=0))


def fill(groups, packets, rows_ref, terms):
    count, width = rows_ref.shape
    cols = width // groups
    group = lax.axis_index("dp")
    parts = [terms[:, at : at + cols] for at in range(0, terms.shape[1], cols)]
    terms = jnp.concatenate(parts, axis=0).astype(BF16)
    for k, packet in enumerate(packets):
        at = pl.ds(pl.multiple_of((group ^ k) * cols, LANES), cols)
        packet[:count, :] = rows_ref[:, at]
        packet[count:, :] = terms


def packet_shape(groups, cent, lat_rows):
    cols = cent.shape[1] // groups
    return shape((cent.shape[0] + TERMS * lat_rows // cols, cols), BF16)


def side(groups, hit, codes, base, enc, cent):
    count, lat_rows = hit.shape
    return pl.pallas_call(
        functools.partial(side_kernel, groups),
        name="side",
        out_shape=(shape((count, lat_rows), F32),) * 2
        + (packet_shape(groups, cent, lat_rows),) * groups,
        in_specs=[VMEM] * 5,
        out_specs=(VMEM,) * (2 + groups),
        compiler_params=params(20),
        cost_estimate=pl.CostEstimate(
            flops=8 * count * lat_rows * 64, bytes_accessed=32 * count * lat_rows, transcendentals=0
        ),
    )(hit, codes, base, enc, cent)


def scores_kernel(rows_dev, act_ref, scores_ref, token_ref):
    token_ref[...] = jnp.zeros_like(token_ref)
    count, lat_rows = act_ref.shape
    block_count = lat_rows // BLK
    me = lax.axis_index("latent")
    latent = lax.broadcasted_iota(jnp.int32, (block_count, lat_rows), 1)
    block = lax.broadcasted_iota(jnp.int32, (block_count, lat_rows), 0)
    inside = jnp.where(latent // BLK == block, 1.0 / BLK, 0.0).astype(F32)
    means = lax.dot_general(
        inside,
        act_ref[...],
        (((1,), (1,)), ((), ())),
        preferred_element_type=F32,
        precision=lax.Precision.HIGHEST,
    )
    at = lax.broadcasted_iota(jnp.int32, (count, count), 0)
    place = lax.broadcasted_iota(jnp.int32, (count, count), 1)
    relative = ((place // rows_dev) ^ me) * rows_dev + place % rows_dev
    order = jnp.where(relative == at, 1.0, 0.0).astype(F32)
    scores_ref[...] = jnp.dot(
        means, order, preferred_element_type=F32, precision=lax.Precision.HIGHEST
    )


def scores(rows_dev, act):
    count, lat_rows = act.shape
    return pl.pallas_call(
        functools.partial(scores_kernel, rows_dev),
        name="scores",
        out_shape=(shape((lat_rows // BLK, count), F32), shape((8, LANES), F32)),
        in_specs=[VMEM],
        out_specs=(VMEM, VMEM),
        compiler_params=params(8),
    )(act)


def exchanged(value, step, mask):
    blocks = range(value.shape[0] // step)
    return jnp.concatenate(
        [value[(k ^ mask) * step : ((k ^ mask) + 1) * step] for k in blocks], axis=0
    )


def combine_kernel(rows_dev, mine_ref, mate_ref, after_ref, sums_ref, sent_ref):
    del after_ref
    sums = mine_ref[...] + exchanged(mate_ref[...], rows_dev, 1)
    sums_ref[...] = sums
    sent_ref[...] = sums.astype(BF16)


def combine(rows_dev, mine, mate, after):
    return pl.pallas_call(
        functools.partial(combine_kernel, rows_dev),
        name="combine",
        out_shape=(shape(mine.shape, F32), shape(mine.shape, BF16)),
        in_specs=[VMEM, VMEM, ANY],
        out_specs=(VMEM, VMEM),
        compiler_params=params(12),
    )(mine, mate, after)


def errors_kernel(rows_dev, dec_ref, input_ref, parts, recon_ref, errors_ref):
    total = parts[0][...]
    for j in range(1, len(parts)):
        total = total + exchanged(parts[j][...].astype(F32), 2 * rows_dev, j)
    full = total + dec_ref[...]
    recon_ref[...] = full[:rows_dev]
    errors_ref[...] = (full - input_ref[...].astype(F32)).astype(BF16)


def backward_kernel(groups, rows_dev, splits, *refs):
    turneds, refs = refs[:splits], refs[splits:]
    cent_ref, codes_ref, base_ref, gate_ref = refs[:4]
    refs = refs[4:]
    second_ref = refs[0]
    if rows_dev:
        chips = cent_ref.shape[0] // (2 * rows_dev)
        dec_ref, input_ref = refs[1:3]
        parts, outs = restored(ORDER, refs[3 : 3 + chips]), refs[3 + chips :]
        recon_ref, packets, errors_ref = outs[0], outs[1:-1], outs[-1]
        errors_kernel(rows_dev, dec_ref, input_ref, parts, recon_ref, errors_ref)
    else:
        errors_ref, packets = refs[1], refs[2:]
    grad = times(errors_ref[...], turneds)
    pre_grad = (grad * gate_ref[...]).astype(BF16).astype(F32)
    codes = codes_ref[...].astype(F32)
    along = jnp.sum(codes * grad + pre_grad * base_ref[...], axis=0, keepdims=True)
    high = along.astype(BF16).astype(F32)
    both = jnp.sum(pre_grad, axis=0, keepdims=True)
    later = jnp.sum(pre_grad * second_ref[...], axis=0, keepdims=True)
    terms = jnp.concatenate([both - later, later, high, along - high], axis=0)
    fill(groups, packets, errors_ref, terms)


def backward(groups, rows_dev, turneds, cent, rest):
    count, width = cent.shape
    lat_rows = rest[0].shape[1]
    packet = packet_shape(groups, cent, lat_rows)
    outs = (packet,) * groups
    scratch = []
    if rows_dev:
        outs = (shape((rows_dev, width), F32),) + outs
        scratch = [pltpu.VMEM((count, width), BF16)]
    return pl.pallas_call(
        functools.partial(backward_kernel, groups, rows_dev, len(turneds)),
        name="backward",
        out_shape=outs,
        in_specs=[VMEM] * (len(turneds) + 1 + len(rest)),
        out_specs=(VMEM,) * len(outs),
        scratch_shapes=scratch,
        compiler_params=params(20),
        cost_estimate=pl.CostEstimate(
            flops=2 * count * lat_rows * width, bytes_accessed=2 * lat_rows * width, transcendentals=0
        ),
    )(*turneds, cent, *rest)


def rounded_kernel(value_ref, out_ref):
    out_ref[...] = value_ref[...].astype(BF16)


def rounded(value):
    return pl.pallas_call(
        rounded_kernel,
        name="rounded",
        out_shape=shape(value.shape, BF16),
        in_specs=[VMEM],
        out_specs=VMEM,
        compiler_params=params(4),
    )(value)


def gradient_kernel(count, given, unit_ref, inverse_ref, *refs):
    out_ref, left_ref, right_ref, held_ref, sems = refs[-5:]
    sides, packets, before_refs = refs[:given], refs[given : 2 * given], refs[2 * given : -5]
    lat_rows, cols = out_ref.shape
    depth = 2 * count * len(packets)
    extra = left_ref.shape[0] - depth
    along = []
    number = (lax.broadcasted_iota(jnp.int32, (count, lat_rows), 0) + 1).astype(F32)
    for g, (known, packet) in enumerate(zip(sides, packets)):
        base = g * 2 * count
        right_ref[base : base + count, :cols] = packet[:count, :]
        right_ref[base + count : base + 2 * count, :cols] = known[:count, :]
        code0, code1, row0, row1 = unfilled(known, count)
        grad0, grad1, *shares = unfilled(packet, count)
        at0, at1 = number == row0, number == row1
        code = jnp.where(at0, code0, jnp.where(at1, code1, 0.0))
        grad = jnp.where(at0, grad0, jnp.where(at1, grad1, 0.0))
        left_ref[base : base + count, :] = code.astype(BF16)
        left_ref[base + count : base + 2 * count, :] = grad.astype(BF16)
        along += shares
    if extra > 2 * len(packets):
        along.append(jnp.zeros((extra - 2 * len(packets), lat_rows), F32))
    left_ref[depth:, :] = jnp.concatenate(along, axis=0).astype(BF16)
    right_ref[depth:, :cols] = jnp.zeros((extra, cols), BF16)
    right_ref[:depth, cols:] = jnp.zeros((depth, LANES), BF16)
    right_ref[depth:, cols:] = jnp.ones((extra, LANES), BF16)
    start = pl.multiple_of(lax.axis_index("dp") * cols, LANES)
    copies = []
    for at in range(lat_rows // LANES):
        rows = pl.ds(at * LANES, LANES)
        outer = lax.dot_general(
            left_ref[:, rows],
            right_ref[...],
            (((0,), (0,)), ((), ())),
            preferred_element_type=F32,
        )
        unit = unit_ref[rows, pl.ds(start, cols)].astype(F32)
        inverse, total = inverse_ref[rows, :], outer[:, cols:]
        for tile in range(0, cols, LANES):
            part = slice(tile, tile + LANES)
            value = (outer[:, part] - unit[:, part] * total) * inverse
            if before_refs:
                held_ref[rows, part] = before_refs[0][rows, part] + value
            else:
                out_ref[rows, part] = value
        if before_refs:
            copies.append(pltpu.make_async_copy(held_ref.at[rows], out_ref.at[rows], sems.at[at]))
            copies[-1].start()
    for copy in copies:
        copy.wait()


def unfilled(packet, count):
    values = packet[count:, :].astype(F32)
    parts = [values[at : at + TERMS] for at in range(0, values.shape[0], TERMS)]
    terms = jnp.concatenate(parts, axis=1)
    return [terms[t : t + 1] for t in range(TERMS)]


def gradient(name, count, unit, inverse, sides, packets, before):
    lat_rows = unit.shape[0]
    cols = packets[0].shape[1]
    depth = 2 * count * len(packets)
    rows = depth + max(16, 2 * len(packets))
    return pl.pallas_call(
        functools.partial(gradient_kernel, count, len(packets)),
        name=name,
        out_shape=shape((lat_rows, cols), F32),
        in_specs=[VMEM] * (2 + 2 * len(packets) + len(before)),
        out_specs=HBM if before else VMEM,
        scratch_shapes=[
            pltpu.VMEM((rows, lat_rows), BF16),
            pltpu.VMEM((rows, cols + LANES), BF16),
            pltpu.VMEM((lat_rows, cols) if before else (8, LANES), F32),
            pltpu.SemaphoreType.DMA((lat_rows // LANES,)),
        ],
        compiler_params=params(24),
        cost_estimate=pl.CostEstimate(
            flops=2 * depth * lat_rows * cols, bytes_accessed=8 * lat_rows * cols, transcendentals=0
        ),
    )(unit, inverse, *sides, *packets, *before)


def local(inputs, blocks, weights, enc_bias, dec_bias):
    rows_dev = inputs.shape[0]
    top = blocks.shape[1]
    chips = lax.axis_size("latent") // 2
    groups = lax.axis_size("dp")
    count = 2 * chips * rows_dev
    dec, enc = dec_bias[None, :], enc_bias[None, :]

    mate, mate_names = swap(inputs, "latent", 1), swap(blocks, "latent", 1)
    width = inputs.shape[1]
    lane = lax.broadcasted_iota(jnp.int32, (rows_dev, width + LANES), 1)
    high = jnp.pad(blocks, ((0, 0), (width, LANES - top)))
    low = jnp.pad(blocks, ((0, 0), (width + top, LANES - 2 * top)))
    lists = jnp.where(lane < width + top, high >> SHIFT, low & (RADIX - 1))
    own = jnp.where(lane < width, jnp.pad(inputs, ((0, 0), (0, LANES))), lists.astype(BF16))
    both = pack(own, mate, mate_names)
    pieces = swaps([both] * chips, "latent", 2)
    unit, turned, inverse = normalize(both, weights)
    units, turneds = [unit], [turned]
    contrib, cent, rows, codes, base, act, hit = forward(
        rows_dev, top, dec, enc, units, turneds, pieces
    )
    block_scores, token = scores(rows_dev, act)
    sums, sent = combine(rows_dev, contrib, swap(contrib, "latent", 1), token)
    gate, second, *sides = side(groups, hit, codes, base, enc, cent)
    sides = swaps(sides, "dp", 1)
    known = (codes, base, gate, second)
    if chips <= DIRECT:
        parts = [sums] + swaps([sent] * chips, "latent", 2)[1:]
        recon, *packets = backward(
            groups, rows_dev, turneds, cent, (*known, dec, rows, *taken(ORDER, parts))
        )
    else:
        full = dec_bias + sums[:rows_dev]
        for j in range(1, chips):
            at = 2 * j * rows_dev
            full = full + swap(sums[at : at + rows_dev], "latent", 2 * j)
        recon = full
        errors = (full - rows[:rows_dev].astype(F32)).astype(BF16)
        errors = jnp.concatenate([errors, swap(errors, "latent", 1)], axis=0)
        errors = jnp.concatenate(swaps([errors] * chips, "latent", 2), axis=0)
        packets = backward(groups, 0, turneds, cent, (*known, errors))
    packets = swaps(packets, "dp", 1)
    late = LATE if groups == len(ORDER) else groups - 1
    early = [k for k in range(groups) if k != late]
    partial = gradient(
        "early", count, unit, inverse, [sides[k] for k in early], [packets[k] for k in early], []
    )
    grad_weights = gradient(
        "gradient", count, unit, inverse, [sides[late]], [packets[late]], [partial]
    )
    return (rounded(recon), grad_weights, block_scores)


def solution(mesh):
    in_specs = (
        P(("dp", "latent"), None),
        P(("dp", "latent"), None),
        P("latent", None),
        P("latent"),
        P(),
    )
    out_specs = (P(("dp", "latent"), None), P("latent", "dp"), P("latent", "dp"))
    return jax.shard_map(local, mesh=mesh, in_specs=in_specs, out_specs=out_specs, check_vma=False)
```
